512 devices in a mesh: gx: 32 (over y, x), gy: 16 (over z, core).
Axes of the slice: x: 4, y: 8, z: 8, core: 2. Of those that a mesh axis runs over, the one named last changes fastest.
Arguments:
- water_state: float32 [3, 2048, 8192], P(None, 'gy', 'gx'), may hold values from -0.5 to 1.5, as said below
- bed_level: float32 [2048, 8192], P('gy', 'gx'), may hold values from -0.1 to 0.1
- active_tiles: int32 [1, 16, 64], replicated, may hold values from 0 to 1, as said below
- roughness: int32 [16, 64], replicated, may hold values from 0 to 3
Outputs:
- water_out: float32 [3, 2048, 8192], P(None, 'gy', 'gx')
The draws below stay inside these ranges and needn't reach their ends.
Inputs may be any that keep to these rules, and one draw needn't show every extreme that they name: `water_state`: entry 0 along the first dimension is the water depth, at least 0.5 everywhere; entries 1 and 2 are the discharges along the columns and along the rows, of magnitude at most 0.5. `active_tiles`: whole blocks of 2 tiles side by side along the columns, starting at multiples of 2, may be off the list together.
All inputs are finite; a program needn't handle non-finite values.
Results may differ from the reference program's by a relative error of at most 0.0003.
Values sent between devices are 32-bit elements; how exact they have to be, the bound alone decides.
No kernel may reach another device: no remote copies, remote signals or barrier semaphores. Data moves between devices by JAX's collectives and lax.ppermute only.
A program may use at most 64 MiB of HBM per device.

```python
import jax
import jax.numpy as jnp
from jax import lax

TILE = 128
TX_DEV = 2
SUBSTEPS = 1
NY = 2048
NX = 8192
NTY = 16
NTX = 64


def draw_water_state(key, part):
    depth_key, flow_key = jax.random.split(key, 2)
    water_depth = jax.random.uniform(depth_key, (NY, NX), jnp.float32, 0.5, 1.5)
    discharge = jax.random.uniform(flow_key, (2, NY, NX), jnp.float32, -0.5, 0.5)
    return jnp.concatenate([water_depth[None], discharge], axis=0)


def draw_active_tiles(key, part):
    block_key, tile_key = jax.random.split(jax.random.fold_in(key, 7))
    block_wet = jax.random.randint(block_key, (SUBSTEPS, NTY, NTX // TX_DEV, 1), 0, 5) < 3
    tile_wet = jax.random.randint(tile_key, (SUBSTEPS, NTY, NTX // TX_DEV, TX_DEV), 0, 4) > 0
    return (block_wet & tile_wet).reshape(SUBSTEPS, NTY, NTX).astype(jnp.int32)


def place_ends(values, own_key, low, top_value):
    longest = values.shape.index(max(values.shape))
    spots = []
    for shift in (0, 1):
        where = [jax.random.randint(jax.random.fold_in(own_key, axis), (), 0, length) for axis, length in enumerate(values.shape)]
        where[longest] = (where[longest] + shift) % values.shape[longest]
        spots.append(tuple(where))
    return values.at[spots[0]].set(low).at[spots[1]].set(top_value)


def levels(stream_key, extent, shards, least, high):
    factor_of, own = 1.0, jax.random.fold_in(stream_key, 6)
    for dim, parts in shards:
        heights = jnp.exp(jax.random.uniform(jax.random.fold_in(own, dim), (parts,), jnp.float32, least / len(shards), high / len(shards)))
        factor_of = factor_of * jnp.repeat(heights, extent[dim] // parts).reshape([-1 if axis == dim else 1 for axis in range(len(extent))])
    return factor_of


def setup_inputs(seed: int = 0) -> dict:
    splits = jax.random.split(jax.random.key(seed), 5)
    water_state = draw_water_state(jax.random.fold_in(splits[4], 71), 0)
    bed_level = jnp.clip(jax.random.uniform(splits[1], (NY, NX), jnp.float32, -0.1, 0.1) * levels(splits[1], (NY, NX), ((0, 16), (1, 32)), -0.4, 0.0), -0.1, 0.1)
    active_tiles = draw_active_tiles(jax.random.fold_in(splits[4], 71), 0)
    roughness = place_ends(jax.random.randint(splits[3], (NTY, NTX), 0, 4), jax.random.fold_in(splits[3], 1), 0, 3).astype(jnp.int32)
    return dict(water_state=water_state, bed_level=bed_level, active_tiles=active_tiles, roughness=roughness)


GRAVITY = 9.81
SPACING = 2.0
TIME_STEP = 0.1
MANNING = (0.03, 0.06, 0.1, 0.15)
ROW_SIGNS = (1.0, 1.0, -1.0)
COL_SIGNS = (1.0, -1.0, 1.0)

def minmod_limit(lower, upper):
    return jnp.where(lower * upper > 0.0, jnp.sign(lower) * jnp.minimum(jnp.abs(lower), jnp.abs(upper)), 0.0)

def cut_along(array, begin, finish, axis):
    return lax.slice_in_dim(array, begin, finish, axis=axis)

def face_states(field, axis, interior):
    between = cut_along(field, 1, interior + 4, axis) - cut_along(field, 0, interior + 3, axis)
    slopes = minmod_limit(cut_along(between, 0, interior + 2, axis), cut_along(between, 1, interior + 3, axis))
    left_side = cut_along(field, 1, interior + 2, axis) + 0.5 * cut_along(slopes, 0, interior + 1, axis)
    right_side = cut_along(field, 2, interior + 3, axis) - 0.5 * cut_along(slopes, 1, interior + 2, axis)
    return (left_side, right_side)

def physical_flux(water_depth, normal_flow, tangent_flow):
    velocity = normal_flow / water_depth
    fluxes = (normal_flow, normal_flow * velocity + 0.5 * GRAVITY * water_depth * water_depth, tangent_flow * velocity)
    return (fluxes, jnp.abs(velocity) + jnp.sqrt(GRAVITY * water_depth))

def rusanov_flux(left_side, right_side):
    left_flux, left_speed = physical_flux(*left_side)
    right_flux, right_speed = physical_flux(*right_side)
    fastest = jnp.maximum(left_speed, right_speed)
    return tuple((0.5 * (a + b) - 0.5 * fastest * (r - l) for a, b, l, r in zip(left_flux, right_flux, left_side, right_side)))

def tendency(extended, bed_part, friction, active, row_count, col_count):
    water_depth, flow_x, flow_y = (extended[0], extended[1], extended[2])
    across = [face_states(f[2:row_count + 2, :], 1, col_count) for f in (water_depth, flow_x, flow_y)]
    flux_x = rusanov_flux(tuple((p[0] for p in across)), tuple((p[1] for p in across)))
    downward = [face_states(f[:, 2:col_count + 2], 0, row_count) for f in (water_depth, flow_y, flow_x)]
    flux_y = rusanov_flux(tuple((p[0] for p in downward)), tuple((p[1] for p in downward)))
    centre_depth = water_depth[2:row_count + 2, 2:col_count + 2]
    centre_x = flow_x[2:row_count + 2, 2:col_count + 2]
    centre_y = flow_y[2:row_count + 2, 2:col_count + 2]
    slope_x = (bed_part[2:row_count + 2, 3:col_count + 3] - bed_part[2:row_count + 2, 1:col_count + 1]) / (2.0 * SPACING)
    slope_y = (bed_part[3:row_count + 3, 2:col_count + 2] - bed_part[1:row_count + 1, 2:col_count + 2]) / (2.0 * SPACING)
    resistance = GRAVITY * friction * jnp.sqrt(centre_x * centre_x + centre_y * centre_y) / (centre_depth * jnp.exp(jnp.log(centre_depth) * (4.0 / 3.0)))

    def along_x(f):
        return (f[:, 1:] - f[:, :-1]) / SPACING

    def along_y(f):
        return (f[1:, :] - f[:-1, :]) / SPACING
    change_depth = -(along_x(flux_x[0]) + along_y(flux_y[0]))
    change_x = -(along_x(flux_x[1]) + along_y(flux_y[2])) - GRAVITY * centre_depth * slope_x - resistance * centre_x
    change_y = -(along_x(flux_x[2]) + along_y(flux_y[1])) - GRAVITY * centre_depth * slope_y - resistance * centre_y
    return jnp.stack([change_depth, change_x, change_y]) * active

def friction_table(roughness):
    table = jnp.zeros(roughness.shape, jnp.float32)
    for level, value in enumerate(MANNING):
        table = table + jnp.where(roughness == level, value * value, 0.0)
    return table

def reflect_pad(field, rim_width, row_sign, col_sign):
    padded = jnp.pad(field, ((rim_width, rim_width), (0, 0)), mode='symmetric')
    places = jnp.arange(padded.shape[0])
    ghost = (places < rim_width) | (places >= padded.shape[0] - rim_width)
    padded = padded * jnp.where(ghost, row_sign, 1.0)[:, None]
    padded = jnp.pad(padded, ((0, 0), (rim_width, rim_width)), mode='symmetric')
    places = jnp.arange(padded.shape[1])
    ghost = (places < rim_width) | (places >= padded.shape[1] - rim_width)
    return padded * jnp.where(ghost, col_sign, 1.0)[None, :]

def grid_tendency(fields, bed_padded, flags, friction):
    padded = jnp.stack([reflect_pad(fields[i], 2, ROW_SIGNS[i], COL_SIGNS[i]) for i in range(3)])

    def row_band(band):
        first_row = band * TILE
        extended = lax.dynamic_slice_in_dim(padded, first_row, TILE + 4, axis=1)
        bed_band = lax.dynamic_slice_in_dim(bed_padded, first_row, TILE + 4, axis=0)
        active = jnp.broadcast_to(jnp.repeat(lax.dynamic_index_in_dim(flags, band, 0, keepdims=False), TILE), (TILE, NX))
        drag_band = jnp.broadcast_to(jnp.repeat(lax.dynamic_index_in_dim(friction, band, 0, keepdims=False), TILE), (TILE, NX))
        return tendency(extended, bed_band, drag_band, active, TILE, NX)
    bands = lax.map(row_band, jnp.arange(NTY, dtype=jnp.int32))
    return jnp.transpose(bands, (1, 0, 2, 3)).reshape(3, NY, NX)

def reference(water_state, bed_level, active_tiles, roughness):
    bed_padded = reflect_pad(bed_level, 2, 1.0, 1.0)
    friction = friction_table(roughness)
    fields = water_state
    for substep in range(SUBSTEPS):
        flags = active_tiles[substep].astype(jnp.float32)
        section_one = fields + TIME_STEP * grid_tendency(fields, bed_padded, flags, friction)
        fields = 0.5 * fields + 0.5 * (section_one + TIME_STEP * grid_tendency(section_one, bed_padded, flags, friction))
    return fields
```

```python
import jax
import jax.numpy as jnp
from jax import lax
from jax.experimental import pallas as pl
from jax.experimental.pallas import tpu as pltpu
from jax.sharding import PartitionSpec as P

GRAVITY = 9.81
SPACING = 2.0
TIME_STEP = 0.1
MANNING = (0.03, 0.06, 0.1, 0.15)

LANES = 128
ROWS = 128
HALO = 4
TOP = 16
STAGED = ROWS + 2 * TOP
RIM = 2
SQRT_G = GRAVITY**0.5
HALF_G = 0.5 * GRAVITY
FLUX_SCALE = 0.5 * TIME_STEP / SPACING
BED_SCALE = TIME_STEP * GRAVITY / (2.0 * SPACING)
DRAG_SCALE = TIME_STEP * GRAVITY

VMEM = pl.BlockSpec(memory_space=pltpu.VMEM)
SMEM = pl.BlockSpec(memory_space=pltpu.SMEM)


def swap(x, axis, odd):
    n = lax.axis_size(axis)
    pairs = []
    for i in range(odd, n - 1, 2):
        pairs += [(i, i + 1), (i + 1, i)]
    return lax.ppermute(x, axis, pairs)


def lane_ids(rows):
    return lax.broadcasted_iota(jnp.int32, (rows, LANES), 1)


def strips_kernel(water, bed, msg_a, msg_b):
    even = lax.rem(lax.axis_index("gx"), 2) == 0
    group = lane_ids(ROWS) // HALO
    packed = None
    for f in range(4):
        for side in range(2):
            cols = pl.ds(side * LANES, LANES)
            v = water[f, :, cols] if f < 3 else bed[:, cols]
            shift = (4 * f + 20 * side) % LANES
            v = pltpu.roll(v, shift, 1) if shift else v
            packed = v if packed is None else jnp.where(group == f + 4 * side, v, packed)
    across = packed.T
    left, right = across[0:16, :], across[16:32, :]
    msg_a[...] = jnp.where(even, right, left)
    msg_b[...] = jnp.where(even, left, right)


def rows_kernel(water, bed, own_b, got_a, got_b, rim, msg_a, msg_b, stage):
    gx, nx = lax.axis_index("gx"), lax.axis_size("gx")
    even = lax.rem(gx, 2) == 0
    border = jnp.logical_or(gx == 0, gx == nx - 1)
    stage[...] = jnp.zeros_like(stage)
    for f in range(4):
        a = got_a[4 * f : 4 * f + 4, :]
        b = got_b[4 * f : 4 * f + 4, :]
        sign = -1.0 if f == 1 else 1.0
        mirrored = jnp.concatenate(
            [own_b[4 * f + 3 - k : 4 * f + 4 - k, :] for k in range(4)], axis=0
        )
        b = jnp.where(border, sign * mirrored, b)
        stage[8 * f : 8 * f + 4, :] = jnp.where(even, b, a)
        stage[8 * f + 4 : 8 * f + 8, :] = jnp.where(even, a, b)
    upright = stage[...].T
    even_y = lax.rem(lax.axis_index("gy"), 2) == 0
    for f in range(4):
        tile = pltpu.roll(upright, 124 - 8 * f, 1)
        rim[f] = tile
        for t in range(3):
            if t == RIM:
                upper, lower = tile[0:4, :], tile[124:128, :]
            else:
                cols = pl.ds(t * LANES, LANES)
                if f < 3:
                    upper, lower = water[f, 0:4, cols], water[f, 124:128, cols]
                else:
                    upper, lower = bed[0:4, cols], bed[124:128, cols]
            at = (pl.ds(4 * f, 4), pl.ds(t * LANES, LANES))
            msg_a[at] = jnp.where(even_y, lower, upper)
            msg_b[at] = jnp.where(even_y, upper, lower)


def minmod_half(a, b):
    return 0.5 * jnp.maximum(jnp.minimum(a, b), jnp.minimum(jnp.maximum(a, b), 0.0))


def side_terms(h, n):
    q = lax.rsqrt(h)
    u = n * (q * q)
    return u, jnp.abs(u) + SQRT_G * (h * q)


def rusanov(left, right):
    (hl, nl, tl), (hr, nr, tr) = left, right
    ul, cl = side_terms(hl, nl)
    ur, cr = side_terms(hr, nr)
    c = jnp.maximum(cl, cr)
    return (
        (nl + nr) - c * (hr - hl),
        (nl * ul + nr * ur) + HALF_G * (hl * hl + hr * hr) - c * (nr - nl),
        (tl * ul + tr * ur) - c * (tr - tl),
    )


def drag(h, p, r):
    return jnp.sqrt(p * p + r * r) * jnp.exp(jnp.log(h) * (-7.0 / 3.0))


class Ring:
    def __init__(self):
        lanes = lane_ids(8)
        self.first = lanes == 0
        self.last = lanes == LANES - 1
        self.low = lanes < 64

    def right(self, v):
        moved = [pltpu.roll(x, 1, 1) for x in v]
        return [jnp.where(self.first, moved[t - 1], moved[t]) for t in range(3)]

    def left(self, v, count=3):
        moved = [pltpu.roll(x, LANES - 1, 1) for x in v]
        return [jnp.where(self.last, moved[(t + 1) % 3], moved[t]) for t in range(count)]

    def rates(self, h, p, r, count):
        before, after = [], []
        for v in (h, p, r):
            moved = self.right(v)
            d = [v[t] - moved[t] for t in range(3)]
            following = self.left(d)
            s = [minmod_half(d[t], following[t]) for t in range(3)]
            after.append([v[t] - s[t] for t in range(3)])
            before.append(self.right([v[t] + s[t] for t in range(3)]))
        face = [
            rusanov([x[t] for x in before], [x[t] for x in after]) for t in range(3)
        ]
        out = []
        for i in range(3):
            g = [face[t][i] for t in range(3)]
            moved = self.left(g, count)
            out.append([moved[t] - g[t] for t in range(count)])
        return out


def row_faces(load, tiles):
    out = []
    for t in tiles:
        upper, lower = [], []
        for f in (0, 2, 1):
            vm, v0, v1, v2 = (load(f, t, k) for k in (-1, 0, 1, 2))
            d0, d1, d2 = v0 - vm, v1 - v0, v2 - v1
            upper.append(v0 + minmod_half(d0, d1))
            lower.append(v1 - minmod_half(d1, d2))
        out.append(rusanov(upper, lower))
    return out


def solve_kernel(active, rough, water, bed, rim, own_b, got_a, got_b, out, held, mid, slope):
    gx, nx = lax.axis_index("gx"), lax.axis_size("gx")
    gy, ny = lax.axis_index("gy"), lax.axis_size("gy")
    even_y = lax.rem(gy, 2) == 0
    border = jnp.logical_or(gy == 0, gy == ny - 1)
    for f in range(4):
        for t in range(3):
            if t == RIM:
                v = rim[f]
            elif f < 3:
                v = water[f, :, pl.ds(t * LANES, LANES)]
            else:
                v = bed[:, pl.ds(t * LANES, LANES)]
            held[3 * f + t, TOP : TOP + ROWS, :] = v
            at = (slice(4 * f, 4 * f + 4), slice(t * LANES, (t + 1) * LANES))
            sign = -1.0 if f == 2 else 1.0
            mirrored = jnp.concatenate(
                [
                    own_b[4 * f + 3 - k : 4 * f + 4 - k, t * LANES : (t + 1) * LANES]
                    for k in range(4)
                ],
                axis=0,
            )
            a = got_a[at]
            b = jnp.where(border, sign * mirrored, got_b[at])
            held[3 * f + t, TOP - 4 : TOP, :] = jnp.where(even_y, b, a)
            held[3 * f + t, TOP + ROWS : TOP + ROWS + 4, :] = jnp.where(even_y, a, b)

    def tile_of(dy, dx):
        row = jnp.clip(gy + dy, 0, ny - 1)
        col = jnp.clip(2 * gx + dx, 0, 2 * nx - 1)
        on = active[0, row, col].astype(jnp.float32)
        level = rough[row, col]
        squares = [DRAG_SCALE * (n * n) for n in MANNING]
        coarse = jnp.where(level == 2, squares[2], squares[3])
        fine = jnp.where(level == 0, squares[0], squares[1])
        return on, jnp.where(level < 2, fine, coarse)

    own = [tile_of(0, 0), tile_of(0, 1)]
    above = [tile_of(-1, 0), tile_of(-1, 1)]
    below = [tile_of(1, 0), tile_of(1, 1)]
    before, after = tile_of(0, -1), tile_of(0, 2)

    ring = Ring()
    rim_pair = [jnp.where(ring.low, after[i], before[i]) for i in range(2)]
    top_row = lax.broadcasted_iota(jnp.int32, (8, LANES), 0) == 0
    bottom_row = lax.broadcasted_iota(jnp.int32, (8, LANES), 0) == 7

    def upper_faces(previous, faces):
        return [
            tuple(
                pltpu.roll(jnp.where(bottom_row, a, b), 1, 0) for a, b in zip(p, n)
            )
            for p, n in zip(previous, faces)
        ]

    def first_stage(c, previous):
        base = pl.multiple_of(8 * c + 8, 8)

        def load(f, t, k):
            return held[3 * f + t, pl.ds(base + k, 8), :]

        faces = row_faces(load, range(3))
        over = upper_faces(previous, faces)
        h, p, r, b = ([load(f, t, 0) for t in range(3)] for f in range(4))
        along = ring.rates(h, p, r, 3)
        to_left, to_right = ring.right(b), ring.left(b)
        for t in range(3):
            if t == RIM:
                on, rub = rim_pair
            else:
                on = jnp.where(c == 0, above[t][0], jnp.where(c == 17, below[t][0], own[t][0]))
                rub = jnp.where(c == 0, above[t][1], jnp.where(c == 17, below[t][1], own[t][1]))
            bed_x = BED_SCALE * (to_right[t] - to_left[t])
            bed_y = BED_SCALE * (load(3, t, 1) - load(3, t, -1))
            if t != RIM:
                slope[t, pl.ds(base, 8), :] = bed_x
                slope[2 + t, pl.ds(base, 8), :] = bed_y
            res = rub * drag(h[t], p[t], r[t])
            down = [n - o for n, o in zip(faces[t], over[t])]
            mid[t, pl.ds(base, 8), :] = h[t] - on * (FLUX_SCALE * (along[0][t] + down[0]))
            mid[3 + t, pl.ds(base, 8), :] = p[t] - on * (
                FLUX_SCALE * (along[1][t] + down[2]) + h[t] * bed_x + res * p[t]
            )
            mid[6 + t, pl.ds(base, 8), :] = r[t] - on * (
                FLUX_SCALE * (along[2][t] + down[1]) + h[t] * bed_y + res * r[t]
            )
        return faces

    zero = jnp.zeros((8, LANES), jnp.float32)
    lax.fori_loop(0, 18, first_stage, [(zero, zero, zero)] * 3)

    def second_load(base):
        return lambda f, t, k: mid[3 * f + t, pl.ds(base + k, 8), :]

    def second_stage(c, previous):
        base = pl.multiple_of(8 * c + TOP, 8)
        load = second_load(base)
        faces = row_faces(load, range(2))
        over = upper_faces(previous, faces)
        h, p, r = ([load(f, t, 0) for t in range(3)] for f in range(3))
        along = ring.rates(h, p, r, 2)
        rows = pl.ds(pl.multiple_of(8 * c, 8), 8)
        for t in range(2):
            on, rub = own[t]
            half = 0.5 * on
            bed_x = slope[t, pl.ds(base, 8), :]
            bed_y = slope[2 + t, pl.ds(base, 8), :]
            res = rub * drag(h[t], p[t], r[t])
            down = [n - o for n, o in zip(faces[t], over[t])]
            change = (
                FLUX_SCALE * (along[0][t] + down[0]),
                FLUX_SCALE * (along[1][t] + down[2]) + h[t] * bed_x + res * p[t],
                FLUX_SCALE * (along[2][t] + down[1]) + h[t] * bed_y + res * r[t],
            )
            for f, v in enumerate((h, p, r)):
                start = held[3 * f + t, pl.ds(base, 8), :]
                out[f, rows, pl.ds(t * LANES, LANES)] = 0.5 * (start + v[t]) - half * change[f]
        return faces

    lax.fori_loop(0, 16, second_stage, row_faces(second_load(TOP - 8), range(2)))


def call(kernel, outs, specs, scratch=()):
    shapes = [jax.ShapeDtypeStruct(s, jnp.float32) for s in outs]
    return pl.pallas_call(
        kernel,
        out_shape=shapes if len(shapes) > 1 else shapes[0],
        in_specs=specs,
        out_specs=[VMEM] * len(shapes) if len(shapes) > 1 else VMEM,
        scratch_shapes=[pltpu.VMEM(s, jnp.float32) for s in scratch],
        name=kernel.__name__,
    )


def body(water, bed, active, rough):
    strip = (16, LANES)
    rows = (16, 3 * LANES)
    col_a, col_b = call(strips_kernel, [strip, strip], [VMEM] * 2)(water, bed)
    got_b = swap(col_b, "gx", 1)
    got_a = swap(col_a, "gx", 0)
    rim, row_a, row_b = call(
        rows_kernel, [(4, ROWS, LANES), rows, rows], [VMEM] * 5, [(LANES, LANES)]
    )(water, bed, col_b, got_a, got_b)
    down_a = swap(row_a, "gy", 0)
    down_b = swap(row_b, "gy", 1)
    return call(
        solve_kernel,
        [(3, ROWS, 2 * LANES)],
        [SMEM, SMEM] + [VMEM] * 6,
        [(12, STAGED, LANES), (9, STAGED, LANES), (4, STAGED, LANES)],
    )(active, rough, water, bed, rim, row_b, down_a, down_b)


def solution(mesh):
    return jax.shard_map(
        body,
        mesh=mesh,
        in_specs=(P(None, "gy", "gx"), P("gy", "gx"), P(), P()),
        out_specs=P(None, "gy", "gx"),
        check_vma=False,
    )
```

```python
import jax
import jax.numpy as jnp
from jax import lax
from jax.experimental import pallas as pl
from jax.experimental.pallas import tpu as pltpu
from jax.sharding import PartitionSpec as P

GRAVITY = 9.81
SPACING = 2.0
TIME_STEP = 0.1
MANNING = (0.03, 0.06, 0.1, 0.15)

LANES = 128
ROWS = 128
HALO = 4
TOP = 16
STAGED = ROWS + 2 * TOP
RIM = 2
SQRT_G = GRAVITY**0.5
HALF_G = 0.5 * GRAVITY
FLUX_SCALE = 0.5 * TIME_STEP / SPACING
BED_SCALE = TIME_STEP * GRAVITY / (2.0 * SPACING)
DRAG_SCALE = TIME_STEP * GRAVITY
SMALLEST = 1.1754944e-38

OWN, ABOVE, BELOW = (0, 1, 2), (3, 4, 2), (5, 6, 2)
REGIONS = 7

VMEM = pl.BlockSpec(memory_space=pltpu.VMEM)
HBM = pl.BlockSpec(memory_space=pltpu.HBM)

HELD = (12, STAGED, LANES)
MID = (9, STAGED, LANES)
SLOPE = (4, STAGED, LANES)
FACTORS = (3 * REGIONS, 8, LANES)
STRIP = (16, LANES)
BAND = (16, 3 * LANES)


def swap(x, axis, odd):
    n = lax.axis_size(axis)
    pairs = []
    for i in range(odd, n - 1, 2):
        pairs += [(i, i + 1), (i + 1, i)]
    return lax.ppermute(x, axis, pairs)


def lane_ids(rows):
    return lax.broadcasted_iota(jnp.int32, (rows, LANES), 1)


def row_ids():
    return lax.broadcasted_iota(jnp.int32, (8, LANES), 0)


def strips_kernel(water, bed, active, rough, msg_b, msg_a, own_b, held, factors, on_flags, levels, sems):
    gx, nx = lax.axis_index("gx"), lax.axis_size("gx")
    gy, ny = lax.axis_index("gy"), lax.axis_size("gy")
    copies = []
    for f in range(4):
        for t in range(2):
            cols = pl.ds(t * LANES, LANES)
            src = water.at[f, :, cols] if f < 3 else bed.at[:, cols]
            dst = held.at[3 * f + t, pl.ds(TOP, ROWS), :]
            copies.append(pltpu.make_async_copy(src, dst, sems.at[len(copies)]))
    copies.append(pltpu.make_async_copy(active, on_flags, sems.at[8]))
    copies.append(pltpu.make_async_copy(rough, levels, sems.at[9]))
    for copy in copies:
        copy.start()
    for copy in copies[:8]:
        copy.wait()

    even = lax.rem(gx, 2) == 0
    group = lane_ids(ROWS) // HALO
    packed = None
    for f in range(4):
        for side in range(2):
            v = held[3 * f + side, TOP : TOP + ROWS, :]
            shift = (4 * f + 20 * side) % LANES
            v = pltpu.roll(v, shift, 1) if shift else v
            packed = v if packed is None else jnp.where(group == f + 4 * side, v, packed)
    across = packed.T
    left, right = across[0:16, :], across[16:32, :]
    msg_a[...] = jnp.where(even, right, left)
    msg_b[...] = jnp.where(even, left, right)
    own_b[...] = jnp.where(even, left, right)

    for copy in copies[8:]:
        copy.wait()

    def tile_of(dy, dx):
        row = jnp.clip(gy + dy, 0, ny - 1)
        col = jnp.clip(2 * gx + dx, 0, 2 * nx - 1)
        on = on_flags[0, row, col].astype(jnp.float32)
        level = levels[row, col]
        squares = [DRAG_SCALE * (n * n) for n in MANNING]
        coarse = jnp.where(level == 2, squares[2], squares[3])
        fine = jnp.where(level == 0, squares[0], squares[1])
        return FLUX_SCALE * on, BED_SCALE * on, jnp.where(level < 2, fine, coarse) * on

    low = lane_ids(8) < 64
    sites = [(0, 0), (0, 1), None, (-1, 0), (-1, 1), (1, 0), (1, 1)]
    for region, site in enumerate(sites):
        if site is None:
            ahead, behind = tile_of(0, 2), tile_of(0, -1)
            values = [jnp.where(low, a, b) for a, b in zip(ahead, behind)]
        else:
            values = [jnp.full((8, LANES), v, jnp.float32) for v in tile_of(*site)]
        for i, v in enumerate(values):
            factors[3 * region + i] = v


def rows_kernel(held_in, own_b, got_b, got_a, msg_b, msg_a, keep_b, held, stage):
    gx, nx = lax.axis_index("gx"), lax.axis_size("gx")
    even = lax.rem(gx, 2) == 0
    border = jnp.logical_or(gx == 0, gx == nx - 1)
    stage[...] = jnp.zeros_like(stage)
    for f in range(4):
        a = got_a[4 * f : 4 * f + 4, :]
        b = got_b[4 * f : 4 * f + 4, :]
        sign = -1.0 if f == 1 else 1.0
        mirrored = jnp.concatenate(
            [own_b[4 * f + 3 - k : 4 * f + 4 - k, :] for k in range(4)], axis=0
        )
        b = jnp.where(border, sign * mirrored, b)
        stage[8 * f : 8 * f + 4, :] = jnp.where(even, b, a)
        stage[8 * f + 4 : 8 * f + 8, :] = jnp.where(even, a, b)
    upright = stage[...].T
    even_y = lax.rem(lax.axis_index("gy"), 2) == 0
    for f in range(4):
        rim = pltpu.roll(upright, 124 - 8 * f, 1)
        held[3 * f + RIM, TOP : TOP + ROWS, :] = rim
        for t in range(3):
            if t == RIM:
                upper, lower = rim[0:4, :], rim[124:128, :]
            else:
                upper = held_in[3 * f + t, TOP : TOP + 4, :]
                lower = held_in[3 * f + t, TOP + 124 : TOP + 128, :]
            at = (pl.ds(4 * f, 4), pl.ds(t * LANES, LANES))
            msg_a[at] = jnp.where(even_y, lower, upper)
            msg_b[at] = jnp.where(even_y, upper, lower)
            keep_b[at] = jnp.where(even_y, upper, lower)


def side_states(vm, v0, v1, v2):
    d0, d1, d2 = v0 - vm, v1 - v0, v2 - v1
    low, high = jnp.minimum(d1, 0.0), jnp.maximum(d1, 0.0)
    s0 = jnp.minimum(jnp.maximum(d0, low), high)
    s1 = jnp.minimum(jnp.maximum(d2, low), high)
    return v0 + 0.5 * s0, v1 - 0.5 * s1


def side_terms(h, n):
    q = lax.rsqrt(h)
    u = n * (q * q)
    return u, jnp.abs(u) + SQRT_G * (h * q)


def rusanov(left, right):
    (hl, nl, tl), (hr, nr, tr) = left, right
    ul, cl = side_terms(hl, nl)
    ur, cr = side_terms(hr, nr)
    c = jnp.maximum(cl, cr)
    return (
        (nl + nr) - c * (hr - hl),
        (nl * ul + nr * ur) + HALF_G * (hl * hl + hr * hr) - c * (nr - nl),
        (tl * ul + tr * ur) - c * (tr - tl),
    )


def drag(h, p, r):
    square = p * p + r * r
    return square * lax.rsqrt(jnp.maximum(square, SMALLEST)) * jnp.exp(jnp.log(h) * (-7.0 / 3.0))


class Ring:
    def __init__(self):
        lanes = lane_ids(8)
        self.first = lanes == 0
        self.second = lanes < 2
        self.last = lanes == LANES - 1

    def right(self, v, by=1):
        moved = [pltpu.roll(x, by, 1) for x in v]
        edge = self.first if by == 1 else self.second
        return [jnp.where(edge, moved[t - 1], moved[t]) for t in range(3)]

    def left(self, v, count=3):
        moved = [pltpu.roll(x, LANES - 1, 1) for x in v]
        return [jnp.where(self.last, moved[(t + 1) % 3], moved[t]) for t in range(count)]

    def rates(self, h, p, r, count):
        sides = []
        for v in (h, p, r):
            near, far, ahead = self.right(v), self.right(v, 2), self.left(v)
            sides.append([side_states(far[t], near[t], v[t], ahead[t]) for t in range(3)])
        face = [
            rusanov([x[t][0] for x in sides], [x[t][1] for x in sides]) for t in range(3)
        ]
        out = []
        for i in range(3):
            g = [face[t][i] for t in range(3)]
            moved = self.left(g, count)
            out.append([moved[t] - g[t] for t in range(count)])
        return out


def row_faces(load, tiles):
    out = []
    for t in tiles:
        sides = [side_states(*(load(f, t, k) for k in (-1, 0, 1, 2))) for f in (0, 2, 1)]
        out.append(rusanov([s[0] for s in sides], [s[1] for s in sides]))
    return out


def upper_faces(previous, faces):
    bottom = row_ids() == 7
    return [
        tuple(pltpu.roll(jnp.where(bottom, a, b), 1, 0) for a, b in zip(p, n))
        for p, n in zip(previous, faces)
    ]


def row_of(c):
    at = 8 * c + TOP - 8
    return at if isinstance(c, int) else pl.multiple_of(at, 8)


def loader(ref, c):
    base = row_of(c)
    return lambda f, t, k: ref[3 * f + t, pl.ds(base + k, 8), :]


def first_stage(ring, held, factors, mid, slope, regions, c, previous):
    rows = pl.ds(row_of(c), 8)
    load = loader(held, c)
    faces = row_faces(load, range(3))
    over = upper_faces(previous, faces)
    h, p, r, b = ([load(f, t, 0) for t in range(3)] for f in range(4))
    along = ring.rates(h, p, r, 3)
    to_left, to_right = ring.right(b), ring.left(b)
    for t in range(3):
        flux, bed, rub = (factors[3 * regions[t] + i] for i in range(3))
        bed_x = bed * (to_right[t] - to_left[t])
        bed_y = bed * (load(3, t, 1) - load(3, t, -1))
        if t != RIM:
            slope[t, rows, :] = bed_x
            slope[2 + t, rows, :] = bed_y
        res = rub * drag(h[t], p[t], r[t])
        down = [n - o for n, o in zip(faces[t], over[t])]
        mid[t, rows, :] = h[t] - flux * (along[0][t] + down[0])
        mid[3 + t, rows, :] = p[t] - (
            flux * (along[1][t] + down[2]) + (h[t] * bed_x + res * p[t])
        )
        mid[6 + t, rows, :] = r[t] - (
            flux * (along[2][t] + down[1]) + (h[t] * bed_y + res * r[t])
        )
    return faces


def second_stage(ring, held, factors, mid, slope, out, c, previous):
    rows = pl.ds(row_of(c), 8)
    load = loader(mid, c)
    faces = row_faces(load, range(2))
    over = upper_faces(previous, faces)
    h, p, r = ([load(f, t, 0) for t in range(3)] for f in range(3))
    along = ring.rates(h, p, r, 2)
    place = 8 * (c - 1)
    for t in range(2):
        flux, _, rub = (factors[3 * OWN[t] + i] for i in range(3))
        res = rub * drag(h[t], p[t], r[t])
        down = [n - o for n, o in zip(faces[t], over[t])]
        change = (
            flux * (along[0][t] + down[0]),
            flux * (along[1][t] + down[2]) + (h[t] * slope[t, rows, :] + res * p[t]),
            flux * (along[2][t] + down[1]) + (h[t] * slope[2 + t, rows, :] + res * r[t]),
        )
        for f, v in enumerate((h, p, r)):
            start = held[3 * f + t, rows, :]
            at = place if isinstance(c, int) else pl.multiple_of(place, 8)
            out[f, pl.ds(at, 8), pl.ds(t * LANES, LANES)] = 0.5 * ((start + v[t]) - change[f])
    return faces


def inner_kernel(held, factors, mid, slope):
    ring = Ring()

    def step(c, previous):
        return first_stage(ring, held, factors, mid, slope, OWN, c, previous)

    lax.fori_loop(2, 16, step, row_faces(loader(held, 1), range(3)), unroll=2)


def outer_kernel(held_in, mid_in, slope_in, factors, own_b, got_b, got_a, out, held, mid, slope):
    gy, ny = lax.axis_index("gy"), lax.axis_size("gy")
    even_y = lax.rem(gy, 2) == 0
    border = jnp.logical_or(gy == 0, gy == ny - 1)
    for f in range(4):
        for t in range(3):
            cols = slice(t * LANES, (t + 1) * LANES)
            sign = -1.0 if f == 2 else 1.0
            mirrored = jnp.concatenate(
                [own_b[4 * f + 3 - k : 4 * f + 4 - k, cols] for k in range(4)], axis=0
            )
            a = got_a[4 * f : 4 * f + 4, cols]
            b = jnp.where(border, sign * mirrored, got_b[4 * f : 4 * f + 4, cols])
            held[3 * f + t, TOP - 4 : TOP, :] = jnp.where(even_y, b, a)
            held[3 * f + t, TOP + ROWS : TOP + ROWS + 4, :] = jnp.where(even_y, a, b)

    ring = Ring()
    zero = jnp.zeros((8, LANES), jnp.float32)

    def one(c, regions, previous):
        return first_stage(ring, held, factors, mid, slope, regions, c, previous)

    one(1, OWN, one(0, ABOVE, [(zero, zero, zero)] * 3))
    one(17, BELOW, one(16, OWN, row_faces(loader(held, 15), range(3))))

    def step(c, previous):
        return second_stage(ring, held, factors, mid, slope, out, c, previous)

    lax.fori_loop(1, 17, step, row_faces(loader(mid, 0), range(2)), unroll=4)


def call(kernel, outs, specs, scratch=(), aliases=None, room=4, cost=0):
    shapes = [jax.ShapeDtypeStruct(s, jnp.float32) for s in outs]
    return pl.pallas_call(
        kernel,
        out_shape=shapes,
        in_specs=specs,
        out_specs=[VMEM] * len(shapes),
        scratch_shapes=scratch,
        input_output_aliases=aliases or {},
        compiler_params=pltpu.CompilerParams(vmem_limit_bytes=room << 20),
        cost_estimate=pl.CostEstimate(flops=cost, bytes_accessed=cost, transcendentals=0),
        name=kernel.__name__,
    )


def body(water, bed, active, rough):
    col_b, col_a, own_col, held, factors = call(
        strips_kernel,
        [STRIP, STRIP, STRIP, HELD, FACTORS],
        [HBM] * 4,
        [
            pltpu.SMEM((1, 16, 64), jnp.int32),
            pltpu.SMEM((16, 64), jnp.int32),
            pltpu.SemaphoreType.DMA((10,)),
        ],
    )(*(pltpu.with_memory_space_constraint(x, pltpu.HBM) for x in (water, bed, active, rough)))
    got_b = swap(col_b, "gx", 1)
    got_a = swap(col_a, "gx", 0)
    row_b, row_a, own_row, held = call(
        rows_kernel,
        [BAND, BAND, BAND, HELD],
        [VMEM] * 4,
        [pltpu.VMEM((LANES, LANES), jnp.float32)],
        {0: 3},
    )(held, own_col, got_b, got_a)
    down_b = swap(row_b, "gy", 1)
    down_a = swap(row_a, "gy", 0)
    mid, slope = call(inner_kernel, [MID, SLOPE], [VMEM] * 2, room=8, cost=10_000_000)(held, factors)
    return call(
        outer_kernel,
        [(3, ROWS, 2 * LANES), HELD, MID, SLOPE],
        [VMEM] * 7,
        aliases={0: 1, 1: 2, 2: 3},
        room=8,
    )(held, mid, slope, factors, own_row, down_b, down_a)[0]


def solution(mesh):
    return jax.shard_map(
        body,
        mesh=mesh,
        in_specs=(P(None, "gy", "gx"), P("gy", "gx"), P(), P()),
        out_specs=P(None, "gy", "gx"),
        check_vma=False,
    )
```

```python
import jax
import jax.numpy as jnp
from jax import lax
from jax.experimental import pallas as pl
from jax.experimental.pallas import tpu as pltpu
from jax.sharding import PartitionSpec as P


GRAVITY = 9.81
SPACING = 2.0
TIME_STEP = 0.1
MANNING = (0.03, 0.06, 0.1, 0.15)

LANES = 128
ROWS = 128
HALO = 4
TOP = 16
STAGED = ROWS + 2 * TOP
RIM = 2
SQRT_G = GRAVITY**0.5
HALF_G = 0.5 * GRAVITY
FLUX_SCALE = 0.5 * TIME_STEP / SPACING
BED_SCALE = TIME_STEP * GRAVITY / (2.0 * SPACING)
DRAG_SCALE = TIME_STEP * GRAVITY
SMALLEST = 1.1754944e-38

OWN, ABOVE, BELOW = (0, 1, 2), (3, 4, 2), (5, 6, 2)
REGIONS = 7

VMEM = pl.BlockSpec(memory_space=pltpu.VMEM)
HBM = pl.BlockSpec(memory_space=pltpu.HBM)

HELD = (12, STAGED, LANES)
MID = (9, STAGED, LANES)
SLOPE = (4, STAGED, LANES)
KNOWN = (8, STAGED, LANES)
FACTORS = (3 * REGIONS, 8, LANES)
STRIP = (16, LANES)
BAND = (16, 3 * LANES)
BLOCK = (3, ROWS, 2 * LANES)
INNER = 16


def swap(x, axis, odd):
    n = lax.axis_size(axis)
    pairs = []
    for i in range(odd, n - 1, 2):
        pairs += [(i, i + 1), (i + 1, i)]
    return lax.ppermute(x, axis, pairs)


def lane_ids(rows):
    return lax.broadcasted_iota(jnp.int32, (rows, LANES), 1)


def row_ids():
    return lax.broadcasted_iota(jnp.int32, (8, LANES), 0)


def strips_kernel(water, bed, msg_b, msg_a, own_b, held, sems):
    even = lax.rem(lax.axis_index("gx"), 2) == 0
    copies = []
    for f in range(4):
        for t in range(2):
            cols = pl.ds(t * LANES, LANES)
            src = water.at[f, :, cols] if f < 3 else bed.at[:, cols]
            dst = held.at[3 * f + t, pl.ds(TOP, ROWS), :]
            copies.append(pltpu.make_async_copy(src, dst, sems.at[len(copies)]))
    for copy in copies:
        copy.start()
    for copy in copies:
        copy.wait()
    group = lane_ids(ROWS) // HALO
    packed = None
    for f in range(4):
        for side in range(2):
            v = held[3 * f + side, TOP : TOP + ROWS, :]
            shift = (4 * f + 20 * side) % LANES
            v = pltpu.roll(v, shift, 1) if shift else v
            packed = v if packed is None else jnp.where(group == f + 4 * side, v, packed)
    across = packed.T
    left, right = across[0:16, :], across[16:32, :]
    msg_a[...] = jnp.where(even, right, left)
    msg_b[...] = jnp.where(even, left, right)
    own_b[...] = jnp.where(even, left, right)


def ahead_kernel(held, active, rough, factors, known, on_flags, levels, sems):
    gx, nx = lax.axis_index("gx"), lax.axis_size("gx")
    gy, ny = lax.axis_index("gy"), lax.axis_size("gy")
    copies = [
        pltpu.make_async_copy(active, on_flags, sems.at[0]),
        pltpu.make_async_copy(rough, levels, sems.at[1]),
    ]
    for copy in copies:
        copy.start()

    def keep_drag(c):
        load = loader(held, c)
        for t in range(2):
            known[6 + t, pl.ds(row_of(c), 8), :] = drag(*(load(f, t, 0) for f in range(3)))

    def ahead(c, previous):
        faces = row_faces(loader(held, c), range(2))
        over = upper_faces(previous, faces)
        for t in range(2):
            for i in range(3):
                known[2 * i + t, pl.ds(row_of(c), 8), :] = faces[t][i] - over[t][i]
        keep_drag(c)
        return faces

    keep_drag(1)
    lax.fori_loop(2, 16, ahead, row_faces(loader(held, 1), range(2)), unroll=2)
    keep_drag(16)
    for copy in copies:
        copy.wait()

    def tile_of(dy, dx):
        row = jnp.clip(gy + dy, 0, ny - 1)
        col = jnp.clip(2 * gx + dx, 0, 2 * nx - 1)
        on = on_flags[0, row, col].astype(jnp.float32)
        level = levels[row, col]
        squares = [DRAG_SCALE * (n * n) for n in MANNING]
        coarse = jnp.where(level == 2, squares[2], squares[3])
        fine = jnp.where(level == 0, squares[0], squares[1])
        return FLUX_SCALE * on, BED_SCALE * on, jnp.where(level < 2, fine, coarse) * on

    low = lane_ids(8) < 64
    sites = [(0, 0), (0, 1), None, (-1, 0), (-1, 1), (1, 0), (1, 1)]
    for region, site in enumerate(sites):
        if site is None:
            ahead, behind = tile_of(0, 2), tile_of(0, -1)
            values = [jnp.where(low, a, b) for a, b in zip(ahead, behind)]
        else:
            values = [jnp.full((8, LANES), v, jnp.float32) for v in tile_of(*site)]
        for i, v in enumerate(values):
            factors[3 * region + i] = v


def rows_kernel(held_in, own_b, got_b, got_a, after, msg_b, msg_a, keep_b, held, stage):
    gx, nx = lax.axis_index("gx"), lax.axis_size("gx")
    even = lax.rem(gx, 2) == 0
    border = jnp.logical_or(gx == 0, gx == nx - 1)
    stage[...] = jnp.zeros_like(stage)
    for f in range(4):
        a = got_a[4 * f : 4 * f + 4, :]
        b = got_b[4 * f : 4 * f + 4, :]
        sign = -1.0 if f == 1 else 1.0
        mirrored = jnp.concatenate(
            [own_b[4 * f + 3 - k : 4 * f + 4 - k, :] for k in range(4)], axis=0
        )
        b = jnp.where(border, sign * mirrored, b)
        stage[8 * f : 8 * f + 4, :] = jnp.where(even, b, a)
        stage[8 * f + 4 : 8 * f + 8, :] = jnp.where(even, a, b)
    upright = stage[...].T
    even_y = lax.rem(lax.axis_index("gy"), 2) == 0
    for f in range(4):
        rim = pltpu.roll(upright, 124 - 8 * f, 1)
        held[3 * f + RIM, TOP : TOP + ROWS, :] = rim
        for t in range(3):
            if t == RIM:
                upper, lower = rim[0:4, :], rim[124:128, :]
            else:
                upper = held_in[3 * f + t, TOP : TOP + 4, :]
                lower = held_in[3 * f + t, TOP + 124 : TOP + 128, :]
            at = (pl.ds(4 * f, 4), pl.ds(t * LANES, LANES))
            msg_a[at] = jnp.where(even_y, lower, upper)
            msg_b[at] = jnp.where(even_y, upper, lower)
            keep_b[at] = jnp.where(even_y, upper, lower)


def side_states(vm, v0, v1, v2):
    d0, d1, d2 = v0 - vm, v1 - v0, v2 - v1
    low, high = jnp.minimum(d1, 0.0), jnp.maximum(d1, 0.0)
    s0 = jnp.minimum(jnp.maximum(d0, low), high)
    s1 = jnp.minimum(jnp.maximum(d2, low), high)
    return v0 + 0.5 * s0, v1 - 0.5 * s1


def side_terms(h, n):
    q = lax.rsqrt(h)
    u = n * (q * q)
    return u, jnp.abs(u) + SQRT_G * (h * q)


def rusanov(left, right):
    (hl, nl, tl), (hr, nr, tr) = left, right
    ul, cl = side_terms(hl, nl)
    ur, cr = side_terms(hr, nr)
    c = jnp.maximum(cl, cr)
    return (
        (nl + nr) - c * (hr - hl),
        (nl * ul + nr * ur) + HALF_G * (hl * hl + hr * hr) - c * (nr - nl),
        (tl * ul + tr * ur) - c * (tr - tl),
    )


def drag(h, p, r):
    square = p * p + r * r
    return square * lax.rsqrt(jnp.maximum(square, SMALLEST)) * jnp.exp(jnp.log(h) * (-7.0 / 3.0))


class Ring:
    def __init__(self):
        lanes = lane_ids(8)
        self.first = lanes == 0
        self.second = lanes < 2
        self.last = lanes == LANES - 1

    def right(self, v, by=1):
        moved = [pltpu.roll(x, by, 1) for x in v]
        edge = self.first if by == 1 else self.second
        return [jnp.where(edge, moved[t - 1], moved[t]) for t in range(3)]

    def left(self, v, count=3):
        moved = [pltpu.roll(x, LANES - 1, 1) for x in v]
        return [jnp.where(self.last, moved[(t + 1) % 3], moved[t]) for t in range(count)]

    def rates(self, h, p, r, count):
        sides = []
        for v in (h, p, r):
            near, far, ahead = self.right(v), self.right(v, 2), self.left(v)
            sides.append([side_states(far[t], near[t], v[t], ahead[t]) for t in range(3)])
        face = [
            rusanov([x[t][0] for x in sides], [x[t][1] for x in sides]) for t in range(3)
        ]
        out = []
        for i in range(3):
            g = [face[t][i] for t in range(3)]
            moved = self.left(g, count)
            out.append([moved[t] - g[t] for t in range(count)])
        return out


def row_faces(load, tiles):
    out = []
    for t in tiles:
        sides = [side_states(*(load(f, t, k) for k in (-1, 0, 1, 2))) for f in (0, 2, 1)]
        out.append(rusanov([s[0] for s in sides], [s[1] for s in sides]))
    return out


def upper_faces(previous, faces):
    bottom = row_ids() == 7
    return [
        tuple(pltpu.roll(jnp.where(bottom, a, b), 1, 0) for a, b in zip(p, n))
        for p, n in zip(previous, faces)
    ]


def row_of(c):
    at = 8 * c + TOP - 8
    return at if isinstance(c, int) else pl.multiple_of(at, 8)


def loader(ref, c):
    base = row_of(c)
    return lambda f, t, k: ref[3 * f + t, pl.ds(base + k, 8), :]


def first_stage(ring, held, factors, mid, slope, regions, c, previous, known=None):
    rows = pl.ds(row_of(c), 8)
    load = loader(held, c)
    faces = row_faces(load, range(3) if known is None else [RIM])
    over = upper_faces(previous, faces)
    downs = [[n - o for n, o in zip(*pair)] for pair in zip(faces, over)]
    if known is not None:
        downs = [[known[2 * i + t, rows, :] for i in range(3)] for t in range(2)] + downs
    h, p, r, b = ([load(f, t, 0) for t in range(3)] for f in range(4))
    along = ring.rates(h, p, r, 3)
    to_left, to_right = ring.right(b), ring.left(b)
    for t in range(3):
        flux, bed, rub = (factors[3 * regions[t] + i] for i in range(3))
        bed_x = bed * (to_right[t] - to_left[t])
        bed_y = bed * (load(3, t, 1) - load(3, t, -1))
        if t != RIM:
            slope[t, rows, :] = bed_x
            slope[2 + t, rows, :] = bed_y
        if known is None or t == RIM:
            res = rub * drag(h[t], p[t], r[t])
        else:
            res = rub * known[6 + t, rows, :]
        down = downs[t]
        mid[t, rows, :] = h[t] - flux * (along[0][t] + down[0])
        mid[3 + t, rows, :] = p[t] - (
            flux * (along[1][t] + down[2]) + (h[t] * bed_x + res * p[t])
        )
        mid[6 + t, rows, :] = r[t] - (
            flux * (along[2][t] + down[1]) + (h[t] * bed_y + res * r[t])
        )
    return faces


def second_stage(ring, held, factors, mid, slope, out, place, c, previous):
    rows = pl.ds(row_of(c), 8)
    load = loader(mid, c)
    faces = row_faces(load, range(2))
    over = upper_faces(previous, faces)
    h, p, r = ([load(f, t, 0) for t in range(3)] for f in range(3))
    along = ring.rates(h, p, r, 2)
    for t in range(2):
        flux, _, rub = (factors[3 * OWN[t] + i] for i in range(3))
        res = rub * drag(h[t], p[t], r[t])
        down = [n - o for n, o in zip(faces[t], over[t])]
        change = (
            flux * (along[0][t] + down[0]),
            flux * (along[1][t] + down[2]) + (h[t] * slope[t, rows, :] + res * p[t]),
            flux * (along[2][t] + down[1]) + (h[t] * slope[2 + t, rows, :] + res * r[t]),
        )
        for f, v in enumerate((h, p, r)):
            start = held[3 * f + t, rows, :]
            out[f, pl.ds(place, 8), pl.ds(t * LANES, LANES)] = 0.5 * ((start + v[t]) - change[f])
    return faces


def inner_section(held, factors, known, mid, slope):
    ring = Ring()

    def first(c, previous):
        return first_stage(ring, held, factors, mid, slope, OWN, c, previous, known)

    lax.fori_loop(2, 16, first, row_faces(loader(held, 1), [RIM]), unroll=2)


def inner_result(held, factors, mid, slope, part):
    ring = Ring()

    def second(c, previous):
        place = pl.multiple_of(8 * c - 8, 8)
        return second_stage(ring, held, factors, mid, slope, part, place, c, previous)

    lax.fori_loop(3, 15, second, row_faces(loader(mid, 2), range(2)), unroll=4)


def odd_kernel(held, factors, known, msg_in, mid, slope, part, msg):
    @pl.when(lax.rem(lax.axis_index("gy"), 2) == 1)
    def _():
        inner_section(held, factors, known, mid, slope)
        inner_result(held, factors, mid, slope, part)


def even_kernel(held, factors, known, msg_in, mid_in, slope_in, mid, slope, msg):
    @pl.when(lax.rem(lax.axis_index("gy"), 2) == 0)
    def _():
        inner_section(held, factors, known, mid, slope)


def rest_kernel(held, factors, mid, slope, part_in, part):
    @pl.when(lax.rem(lax.axis_index("gy"), 2) == 0)
    def _():
        inner_result(held, factors, mid, slope, part)


def outer_kernel(
    held_in, mid_in, slope_in, part, factors, own_b, got_b, got_a, out, held, mid, slope, edge, sems
):
    inner = pl.ds(INNER, ROWS - 2 * INNER)
    copies = [pltpu.make_async_copy(part.at[:, inner, :], out.at[:, inner, :], sems.at[0])]
    for i in range(2):
        src, dst = pl.ds(i * INNER, INNER), pl.ds(i * (ROWS - INNER), INNER)
        copies.append(pltpu.make_async_copy(edge.at[:, src, :], out.at[:, dst, :], sems.at[1 + i]))
    copies[0].start()
    gy, ny = lax.axis_index("gy"), lax.axis_size("gy")
    even_y = lax.rem(gy, 2) == 0
    border = jnp.logical_or(gy == 0, gy == ny - 1)
    for f in range(4):
        for t in range(3):
            cols = slice(t * LANES, (t + 1) * LANES)
            sign = -1.0 if f == 2 else 1.0
            mirrored = jnp.concatenate(
                [own_b[4 * f + 3 - k : 4 * f + 4 - k, cols] for k in range(4)], axis=0
            )
            a = got_a[4 * f : 4 * f + 4, cols]
            b = jnp.where(border, sign * mirrored, got_b[4 * f : 4 * f + 4, cols])
            held[3 * f + t, TOP - 4 : TOP, :] = jnp.where(even_y, b, a)
            held[3 * f + t, TOP + ROWS : TOP + ROWS + 4, :] = jnp.where(even_y, a, b)

    ring = Ring()
    zero = jnp.zeros((8, LANES), jnp.float32)

    def first(c, regions, previous):
        return first_stage(ring, held, factors, mid, slope, regions, c, previous)

    def second(c, place, previous):
        return second_stage(ring, held, factors, mid, slope, edge, place, c, previous)

    first(1, OWN, first(0, ABOVE, [(zero, zero, zero)] * 3))
    first(17, BELOW, first(16, OWN, row_faces(loader(held, 15), range(3))))
    second(2, 8, second(1, 0, row_faces(loader(mid, 0), range(2))))
    copies[1].start()
    second(16, 24, second(15, 16, row_faces(loader(mid, 14), range(2))))
    copies[2].start()
    for copy in copies:
        copy.wait()


def call(kernel, outs, specs, scratch=(), aliases=None, room=4, cost=0, out_specs=None):
    shapes = [jax.ShapeDtypeStruct(s, jnp.float32) for s in outs]
    return pl.pallas_call(
        kernel,
        out_shape=shapes,
        in_specs=specs,
        out_specs=out_specs or [VMEM] * len(shapes),
        scratch_shapes=scratch,
        input_output_aliases=aliases or {},
        compiler_params=pltpu.CompilerParams(vmem_limit_bytes=room << 20),
        cost_estimate=pl.CostEstimate(flops=cost, bytes_accessed=cost, transcendentals=0),
    )


def body(water, bed, active, rough):
    col_b, col_a, own_col, held = call(
        strips_kernel,
        [STRIP, STRIP, STRIP, HELD],
        [HBM] * 2,
        [pltpu.SemaphoreType.DMA((8,))],
    )(*(pltpu.with_memory_space_constraint(x, pltpu.HBM) for x in (water, bed)))
    got_b = swap(col_b, "gx", 1)
    got_a = swap(col_a, "gx", 0)
    factors, known = call(
        ahead_kernel,
        [FACTORS, KNOWN],
        [VMEM, HBM, HBM],
        [
            pltpu.SMEM((1, 16, 64), jnp.int32),
            pltpu.SMEM((16, 64), jnp.int32),
            pltpu.SemaphoreType.DMA((2,)),
        ],
        cost=4_000_000,
    )(held, *(pltpu.with_memory_space_constraint(x, pltpu.HBM) for x in (active, rough)))
    row_b, row_a, own_row, held = call(
        rows_kernel,
        [BAND, BAND, BAND, HELD],
        [VMEM] * 5,
        [pltpu.VMEM((LANES, LANES), jnp.float32)],
        {0: 3},
    )(held, own_col, got_b, got_a, factors)
    mid, slope, part, row_b = call(
        odd_kernel, [MID, SLOPE, BLOCK, BAND], [VMEM] * 4, aliases={3: 3}, room=8, cost=10_000_000
    )(held, factors, known, row_b)
    down_b = swap(row_b, "gy", 1)
    mid, slope, row_a = call(
        even_kernel,
        [MID, SLOPE, BAND],
        [VMEM] * 6,
        aliases={4: 0, 5: 1, 3: 2},
        room=8,
        cost=10_000_000,
    )(held, factors, known, row_a, mid, slope)
    down_a = swap(row_a, "gy", 0)
    part = call(rest_kernel, [BLOCK], [VMEM] * 5, aliases={4: 0}, room=8, cost=10_000_000)(
        held, factors, mid, slope, part
    )[0]
    return call(
        outer_kernel,
        [BLOCK, HELD, MID, SLOPE],
        [VMEM] * 8,
        [pltpu.VMEM((3, 2 * INNER, 2 * LANES), jnp.float32), pltpu.SemaphoreType.DMA((3,))],
        aliases={0: 1, 1: 2, 2: 3},
        room=8,
        out_specs=[HBM] + [VMEM] * 3,
    )(held, mid, slope, part, factors, own_row, down_b, down_a)[0]


def solution(mesh):
    return jax.shard_map(
        body,
        mesh=mesh,
        in_specs=(P(None, "gy", "gx"), P("gy", "gx"), P(), P()),
        out_specs=P(None, "gy", "gx"),
        check_vma=False,
    )
```

```python
import jax
import jax.numpy as jnp
from jax import lax
from jax.experimental import pallas as pl
from jax.experimental.pallas import tpu as pltpu
from jax.sharding import PartitionSpec as P


GRAVITY = 9.81
SPACING = 2.0
TIME_STEP = 0.1
MANNING = (0.03, 0.06, 0.1, 0.15)

LANES = 128
ROWS = 128
HALO = 4
TOP = 16
STAGED = ROWS + 2 * TOP
RIM = 2
SQRT_G = GRAVITY**0.5
HALF_G = 0.5 * GRAVITY
FLUX_SCALE = 0.5 * TIME_STEP / SPACING
BED_SCALE = TIME_STEP * GRAVITY / (2.0 * SPACING)
DRAG_SCALE = TIME_STEP * GRAVITY
SMALLEST = 1.1754944e-38

OWN, EDGES = (0, 1, 2), (3, 4, 2)
REGIONS = 5

VMEM = pl.BlockSpec(memory_space=pltpu.VMEM)
HBM = pl.BlockSpec(memory_space=pltpu.HBM)

HELD = (12, STAGED, LANES)
MID = (9, STAGED, LANES)
SLOPE = (4, STAGED, LANES)
KNOWN = (8, STAGED, LANES)
FACTORS = (3 * REGIONS, 8, LANES)
STRIP = (16, LANES)
BAND = (16, 3 * LANES)
BLOCK = (3, ROWS, 2 * LANES)
EDGE = 8
HALF = 8


def swap(x, axis, odd):
    n = lax.axis_size(axis)
    pairs = []
    for i in range(odd, n - 1, 2):
        pairs += [(i, i + 1), (i + 1, i)]
    return lax.ppermute(x, axis, pairs)


def lane_ids(rows):
    return lax.broadcasted_iota(jnp.int32, (rows, LANES), 1)


def row_ids():
    return lax.broadcasted_iota(jnp.int32, (8, LANES), 0)


def strips_kernel(water, bed, msg_b, msg_a, own_b, held, sems):
    even = lax.rem(lax.axis_index("gx"), 2) == 0
    copies = []
    for f in range(4):
        for t in range(2):
            cols = pl.ds(t * LANES, LANES)
            src = water.at[f, :, cols] if f < 3 else bed.at[:, cols]
            dst = held.at[3 * f + t, pl.ds(TOP, ROWS), :]
            copies.append(pltpu.make_async_copy(src, dst, sems.at[len(copies)]))
    for copy in copies:
        copy.start()
    for copy in copies:
        copy.wait()
    group = lane_ids(ROWS) // HALO
    packed = None
    for f in range(4):
        for side in range(2):
            v = held[3 * f + side, TOP : TOP + ROWS, :]
            shift = (4 * f + 20 * side) % LANES
            v = pltpu.roll(v, shift, 1) if shift else v
            packed = v if packed is None else jnp.where(group == f + 4 * side, v, packed)
    across = packed.T
    left, right = across[0:16, :], across[16:32, :]
    msg_a[...] = jnp.where(even, right, left)
    msg_b[...] = jnp.where(even, left, right)
    own_b[...] = jnp.where(even, left, right)


def ahead_kernel(held, active, rough, factors, known, on_flags, levels, sems):
    gx, nx = lax.axis_index("gx"), lax.axis_size("gx")
    gy, ny = lax.axis_index("gy"), lax.axis_size("gy")
    copies = [
        pltpu.make_async_copy(active, on_flags, sems.at[0]),
        pltpu.make_async_copy(rough, levels, sems.at[1]),
    ]
    for copy in copies:
        copy.start()

    def ahead(c, previous):
        rows = pl.ds(row_of(c), 8)
        load = loader(held, c)
        faces = row_faces(load, range(2))
        over = upper_faces(previous, faces)
        for t in range(2):
            for i in range(3):
                known[2 * i + t, rows, :] = faces[t][i] - over[t][i]
            known[6 + t, rows, :] = drag(*(load(f, t, 0) for f in range(3)))
        return faces

    lax.fori_loop(1, 17, ahead, no_faces(2), unroll=4)
    for copy in copies:
        copy.wait()

    def tile_of(dy, dx):
        row = jnp.clip(gy + dy, 0, ny - 1)
        col = jnp.clip(2 * gx + dx, 0, 2 * nx - 1)
        on = on_flags[0, row, col].astype(jnp.float32)
        level = levels[row, col]
        squares = [DRAG_SCALE * (n * n) for n in MANNING]
        coarse = jnp.where(level == 2, squares[2], squares[3])
        fine = jnp.where(level == 0, squares[0], squares[1])
        return FLUX_SCALE * on, BED_SCALE * on, jnp.where(level < 2, fine, coarse) * on

    def keep(region, values):
        for i, v in enumerate(values):
            factors[3 * region + i] = jnp.broadcast_to(v, (8, LANES))

    rows, low = row_ids(), lane_ids(8) < 64
    for t in range(2):
        own, above, below = tile_of(0, t), tile_of(-1, t), tile_of(1, t)
        keep(OWN[t], own)
        edges = [jnp.where(rows < 4, b, a) for a, b in zip(above, below)]
        outside = jnp.logical_and(rows >= 2, rows < 6)
        keep(EDGES[t], [jnp.where(outside, e, o) for e, o in zip(edges, own)])
    keep(RIM, [jnp.where(low, a, b) for a, b in zip(tile_of(0, 2), tile_of(0, -1))])


def rows_kernel(held_in, own_b, got_b, got_a, after, msg_b, msg_a, keep_b, held, stage):
    gx, nx = lax.axis_index("gx"), lax.axis_size("gx")
    even = lax.rem(gx, 2) == 0
    border = jnp.logical_or(gx == 0, gx == nx - 1)
    stage[...] = jnp.zeros_like(stage)
    for f in range(4):
        a = got_a[4 * f : 4 * f + 4, :]
        b = got_b[4 * f : 4 * f + 4, :]
        sign = -1.0 if f == 1 else 1.0
        mirrored = jnp.concatenate(
            [own_b[4 * f + 3 - k : 4 * f + 4 - k, :] for k in range(4)], axis=0
        )
        b = jnp.where(border, sign * mirrored, b)
        stage[8 * f : 8 * f + 4, :] = jnp.where(even, b, a)
        stage[8 * f + 4 : 8 * f + 8, :] = jnp.where(even, a, b)
    upright = stage[...].T
    even_y = lax.rem(lax.axis_index("gy"), 2) == 0
    for f in range(4):
        rim = pltpu.roll(upright, 124 - 8 * f, 1)
        held[3 * f + RIM, TOP : TOP + ROWS, :] = rim
        for t in range(3):
            if t == RIM:
                upper, lower = rim[0:4, :], rim[124:128, :]
            else:
                upper = held_in[3 * f + t, TOP : TOP + 4, :]
                lower = held_in[3 * f + t, TOP + 124 : TOP + 128, :]
            at = (pl.ds(4 * f, 4), pl.ds(t * LANES, LANES))
            msg_a[at] = jnp.where(even_y, lower, upper)
            msg_b[at] = jnp.where(even_y, upper, lower)
            keep_b[at] = jnp.where(even_y, upper, lower)


def side_states(vm, v0, v1, v2):
    d0, d1, d2 = v0 - vm, v1 - v0, v2 - v1
    low, high = jnp.minimum(d1, 0.0), jnp.maximum(d1, 0.0)
    s0 = jnp.minimum(jnp.maximum(d0, low), high)
    s1 = jnp.minimum(jnp.maximum(d2, low), high)
    return v0 + 0.5 * s0, v1 - 0.5 * s1


def side_terms(h, n):
    q = lax.rsqrt(h)
    u = n * (q * q)
    return u, jnp.abs(u) + SQRT_G * (h * q)


def rusanov(left, right):
    (hl, nl, tl), (hr, nr, tr) = left, right
    ul, cl = side_terms(hl, nl)
    ur, cr = side_terms(hr, nr)
    c = jnp.maximum(cl, cr)
    return (
        (nl + nr) - c * (hr - hl),
        (nl * ul + nr * ur) + HALF_G * (hl * hl + hr * hr) - c * (nr - nl),
        (tl * ul + tr * ur) - c * (tr - tl),
    )


def drag(h, p, r):
    square = p * p + r * r
    return square * lax.rsqrt(jnp.maximum(square, SMALLEST)) * jnp.exp(jnp.log(h) * (-7.0 / 3.0))


class Ring:
    def __init__(self):
        lanes = lane_ids(8)
        self.first = lanes == 0
        self.second = lanes < 2
        self.last = lanes == LANES - 1

    def right(self, v, by=1):
        moved = [pltpu.roll(x, by, 1) for x in v]
        edge = self.first if by == 1 else self.second
        return [jnp.where(edge, moved[t - 1], moved[t]) for t in range(3)]

    def left(self, v, count=3):
        moved = [pltpu.roll(x, LANES - 1, 1) for x in v]
        return [jnp.where(self.last, moved[(t + 1) % 3], moved[t]) for t in range(count)]

    def rates(self, h, p, r, count):
        sides = []
        for v in (h, p, r):
            near, far, ahead = self.right(v), self.right(v, 2), self.left(v)
            sides.append([side_states(far[t], near[t], v[t], ahead[t]) for t in range(3)])
        face = [
            rusanov([x[t][0] for x in sides], [x[t][1] for x in sides]) for t in range(3)
        ]
        out = []
        for i in range(3):
            g = [face[t][i] for t in range(3)]
            moved = self.left(g, count)
            out.append([moved[t] - g[t] for t in range(count)])
        return out


def row_faces(load, tiles, shift=0):
    out = []
    for t in tiles:
        sides = [side_states(*(load(f, t, k + shift) for k in (-1, 0, 1, 2))) for f in (0, 2, 1)]
        out.append(rusanov([s[0] for s in sides], [s[1] for s in sides]))
    return out


def no_faces(count):
    return [(jnp.zeros((8, LANES), jnp.float32),) * 3] * count


def upper_faces(previous, faces):
    bottom = row_ids() == 7
    return [
        tuple(pltpu.roll(jnp.where(bottom, a, b), 1, 0) for a, b in zip(p, n))
        for p, n in zip(previous, faces)
    ]


def differences(faces, over):
    return [[n - o for n, o in zip(*pair)] for pair in zip(faces, over)]


def row_of(c):
    return pl.multiple_of(8 * c + TOP - 8, 8)


def loader(ref, c):
    base = row_of(c)
    return lambda f, t, k: ref[3 * f + t, pl.ds(base + k, 8), :]


def pair_of(ref, e, low, high):
    first, then = ref[e, low : low + 8, :], ref[e, high - 4 : high + 4, :]
    return jnp.where(row_ids() < 4, first, then)


def section(ring, load, downs, factors, regions, drags):
    h, p, r, b = ([load(f, t, 0) for t in range(3)] for f in range(4))
    along = ring.rates(h, p, r, 3)
    to_left, to_right = ring.right(b), ring.left(b)
    states, slopes = [], []
    for t in range(3):
        flux, bed, rub = (factors[3 * regions[t] + i] for i in range(3))
        bed_x = bed * (to_right[t] - to_left[t])
        bed_y = bed * (load(3, t, 1) - load(3, t, -1))
        res = rub * (drag(h[t], p[t], r[t]) if drags[t] is None else drags[t])
        down = downs[t]
        states.append(
            (
                h[t] - flux * (along[0][t] + down[0]),
                p[t] - (flux * (along[1][t] + down[2]) + (h[t] * bed_x + res * p[t])),
                r[t] - (flux * (along[2][t] + down[1]) + (h[t] * bed_y + res * r[t])),
            )
        )
        slopes.append((bed_x, bed_y))
    return states, slopes


def result(ring, load, downs, factors, slope_at, start_at):
    h, p, r = ([load(f, t, 0) for t in range(3)] for f in range(3))
    along = ring.rates(h, p, r, 2)
    out = []
    for t in range(2):
        flux, rub = factors[3 * OWN[t]], factors[3 * OWN[t] + 2]
        res = rub * drag(h[t], p[t], r[t])
        down = downs[t]
        change = (
            flux * (along[0][t] + down[0]),
            flux * (along[1][t] + down[2]) + (h[t] * slope_at(t) + res * p[t]),
            flux * (along[2][t] + down[1]) + (h[t] * slope_at(2 + t) + res * r[t]),
        )
        out.append(
            [0.5 * ((start_at(3 * f + t) + v[t]) - change[f]) for f, v in enumerate((h, p, r))]
        )
    return out


def inner_section(held, factors, known, mid, slope):
    ring = Ring()

    def step(c, previous):
        rows = pl.ds(row_of(c), 8)
        load = loader(held, c)
        faces = row_faces(load, [RIM])
        downs = [[known[2 * i + t, rows, :] for i in range(3)] for t in range(2)]
        downs += differences(faces, upper_faces(previous, faces))
        drags = [known[6, rows, :], known[7, rows, :], None]
        states, slopes = section(ring, load, downs, factors, OWN, drags)
        for t in range(3):
            for f in range(3):
                mid[3 * f + t, rows, :] = states[t][f]
            if t != RIM:
                slope[t, rows, :], slope[2 + t, rows, :] = slopes[t]
        return faces

    lax.fori_loop(1, 17, step, no_faces(1), unroll=4)


def inner_result(held, factors, mid, slope, part, first, last):
    ring = Ring()

    def step(c, previous):
        rows = pl.ds(row_of(c), 8)
        load = loader(mid, c)
        faces = row_faces(load, range(2))
        downs = differences(faces, upper_faces(previous, faces))
        values = result(
            ring, load, downs, factors, lambda i: slope[i, rows, :], lambda e: held[e, rows, :]
        )
        place = pl.ds(pl.multiple_of(8 * c - 8, 8), 8)
        for t in range(2):
            for f in range(3):
                part[f, place, pl.ds(t * LANES, LANES)] = values[t][f]
        return faces

    before = no_faces(2) if first == 1 else row_faces(loader(mid, first - 1), range(2))
    lax.fori_loop(first, last + 1, step, before, unroll=4)


def odd_kernel(held, factors, known, msg_in, mid, slope, part, msg):
    @pl.when(lax.rem(lax.axis_index("gy"), 2) == 1)
    def _():
        inner_section(held, factors, known, mid, slope)
        inner_result(held, factors, mid, slope, part, 1, HALF)


def even_kernel(held, factors, known, msg_in, mid_in, slope_in, part_in, mid, slope, part, msg):
    @pl.when(lax.rem(lax.axis_index("gy"), 2) == 0)
    def _():
        inner_section(held, factors, known, mid, slope)
        inner_result(held, factors, mid, slope, part, 1, HALF)


def rest_kernel(held, factors, mid, slope, part_in, part):
    inner_result(held, factors, mid, slope, part, HALF + 1, 16)


def outer_kernel(
    held_in, mid_in, slope_in, part, factors, own_b, got_b, got_a, out, held, mid, slope, edge, sems
):
    inner = pl.ds(EDGE, ROWS - 2 * EDGE)
    copies = [pltpu.make_async_copy(part.at[:, inner, :], out.at[:, inner, :], sems.at[0])]
    for i in range(2):
        rows = pl.ds(i * (ROWS - EDGE), EDGE)
        copies.append(pltpu.make_async_copy(edge.at[i], out.at[:, rows, :], sems.at[1 + i]))
    copies[0].start()
    gy, ny = lax.axis_index("gy"), lax.axis_size("gy")
    even_y = lax.rem(gy, 2) == 0
    border = jnp.logical_or(gy == 0, gy == ny - 1)
    for f in range(4):
        for t in range(3):
            cols = slice(t * LANES, (t + 1) * LANES)
            sign = -1.0 if f == 2 else 1.0
            mirrored = jnp.concatenate(
                [own_b[4 * f + 3 - k : 4 * f + 4 - k, cols] for k in range(4)], axis=0
            )
            a = got_a[4 * f : 4 * f + 4, cols]
            b = jnp.where(border, sign * mirrored, got_b[4 * f : 4 * f + 4, cols])
            held[3 * f + t, TOP - 4 : TOP, :] = jnp.where(even_y, b, a)
            held[3 * f + t, TOP + ROWS : TOP + ROWS + 4, :] = jnp.where(even_y, a, b)

    ring = Ring()
    end = TOP + ROWS

    def load(f, t, k):
        return pair_of(held, 3 * f + t, end - 2 + k, TOP - 2 + k)

    downs = differences(row_faces(load, range(3)), row_faces(load, range(3), -1))
    states, slopes = section(ring, load, downs, factors, EDGES, [None] * 3)

    def put(ref, e, v):
        ref[e, end - 2 : end + 2, :] = v[0:4, :]
        ref[e, TOP - 2 : TOP + 2, :] = v[4:8, :]

    for t in range(3):
        for f in range(3):
            put(mid, 3 * f + t, states[t][f])
        if t != RIM:
            put(slope, t, slopes[t][0])
            put(slope, 2 + t, slopes[t][1])

    def load_mid(f, t, k):
        return pair_of(mid, 3 * f + t, end - 4 + k, TOP + k)

    downs = differences(row_faces(load_mid, range(2)), row_faces(load_mid, range(2), -1))
    values = result(
        ring,
        load_mid,
        downs,
        factors,
        lambda i: pair_of(slope, i, end - 4, TOP),
        lambda e: pair_of(held, e, end - 4, TOP),
    )
    upper = row_ids() < 4
    for t in range(2):
        cols = pl.ds(t * LANES, LANES)
        for f in range(3):
            v = pltpu.roll(values[t][f], 4, 0)
            edge[0, f, :, cols] = jnp.where(upper, v, part[f, 0:EDGE, cols])
            edge[1, f, :, cols] = jnp.where(upper, part[f, ROWS - EDGE : ROWS, cols], v)
    for copy in copies[1:]:
        copy.start()
    for copy in copies:
        copy.wait()


def call(kernel, outs, specs, scratch=(), aliases=None, room=4, cost=0, out_specs=None):
    shapes = [jax.ShapeDtypeStruct(s, jnp.float32) for s in outs]
    return pl.pallas_call(
        kernel,
        out_shape=shapes,
        in_specs=specs,
        out_specs=out_specs or [VMEM] * len(shapes),
        scratch_shapes=scratch,
        input_output_aliases=aliases or {},
        compiler_params=pltpu.CompilerParams(vmem_limit_bytes=room << 20),
        cost_estimate=pl.CostEstimate(flops=cost, bytes_accessed=cost, transcendentals=0),
    )


def body(water, bed, active, rough):
    col_b, col_a, own_col, held = call(
        strips_kernel,
        [STRIP, STRIP, STRIP, HELD],
        [HBM] * 2,
        [pltpu.SemaphoreType.DMA((8,))],
    )(*(pltpu.with_memory_space_constraint(x, pltpu.HBM) for x in (water, bed)))
    got_b = swap(col_b, "gx", 1)
    got_a = swap(col_a, "gx", 0)
    factors, known = call(
        ahead_kernel,
        [FACTORS, KNOWN],
        [VMEM, HBM, HBM],
        [
            pltpu.SMEM((1, 16, 64), jnp.int32),
            pltpu.SMEM((16, 64), jnp.int32),
            pltpu.SemaphoreType.DMA((2,)),
        ],
        cost=4_000_000,
    )(held, *(pltpu.with_memory_space_constraint(x, pltpu.HBM) for x in (active, rough)))
    row_b, row_a, own_row, held = call(
        rows_kernel,
        [BAND, BAND, BAND, HELD],
        [VMEM] * 5,
        [pltpu.VMEM((LANES, LANES), jnp.float32)],
        {0: 3},
    )(held, own_col, got_b, got_a, factors)
    mid, slope, part, row_b = call(
        odd_kernel, [MID, SLOPE, BLOCK, BAND], [VMEM] * 4, aliases={3: 3}, room=8, cost=10_000_000
    )(held, factors, known, row_b)
    down_b = swap(row_b, "gy", 1)
    mid, slope, part, row_a = call(
        even_kernel,
        [MID, SLOPE, BLOCK, BAND],
        [VMEM] * 7,
        aliases={4: 0, 5: 1, 6: 2, 3: 3},
        room=8,
        cost=10_000_000,
    )(held, factors, known, row_a, mid, slope, part)
    down_a = swap(row_a, "gy", 0)
    part = call(rest_kernel, [BLOCK], [VMEM] * 5, aliases={4: 0}, room=8, cost=10_000_000)(
        held, factors, mid, slope, part
    )[0]
    return call(
        outer_kernel,
        [BLOCK, HELD, MID, SLOPE],
        [VMEM] * 8,
        [pltpu.VMEM((2, 3, EDGE, 2 * LANES), jnp.float32), pltpu.SemaphoreType.DMA((3,))],
        aliases={0: 1, 1: 2, 2: 3},
        room=8,
        out_specs=[HBM] + [VMEM] * 3,
    )(held, mid, slope, part, factors, own_row, down_b, down_a)[0]


def solution(mesh):
    return jax.shard_map(
        body,
        mesh=mesh,
        in_specs=(P(None, "gy", "gx"), P("gy", "gx"), P(), P()),
        out_specs=P(None, "gy", "gx"),
        check_vma=False,
    )
```

```python
import jax
import jax.numpy as jnp
from jax import lax
from jax.experimental import pallas as pl
from jax.experimental.pallas import tpu as pltpu
from jax.sharding import PartitionSpec as P


GRAVITY = 9.81
SPACING = 2.0
TIME_STEP = 0.1
MANNING = (0.03, 0.06, 0.1, 0.15)

LANES = 128
ROWS = 128
HALO = 4
TOP = 16
STAGED = ROWS + 2 * TOP
RIM = 2
SQRT_G = GRAVITY**0.5
HALF_G = 0.5 * GRAVITY
FLUX_SCALE = 0.5 * TIME_STEP / SPACING
BED_SCALE = TIME_STEP * GRAVITY / (2.0 * SPACING)
DRAG_SCALE = TIME_STEP * GRAVITY
SMALLEST = 1.1754944e-38

OWN, EDGES = (0, 1, 2), (3, 4, 2)
REGIONS = 5

VMEM = pl.BlockSpec(memory_space=pltpu.VMEM)
HBM = pl.BlockSpec(memory_space=pltpu.HBM)

HELD = (12, STAGED, LANES)
MID = (9, STAGED, LANES)
SLOPE = (4, STAGED, LANES)
KNOWN = (8, STAGED, LANES)
FACTORS = (3 * REGIONS, 8, LANES)
STRIP = (16, LANES)
BAND = (16, 3 * LANES)
BLOCK = (3, ROWS, 2 * LANES)
EDGE = 8
FIRST = 4


def swap(x, axis, odd):
    n = lax.axis_size(axis)
    pairs = []
    for i in range(odd, n - 1, 2):
        pairs += [(i, i + 1), (i + 1, i)]
    return lax.ppermute(x, axis, pairs)


def lane_ids(rows):
    return lax.broadcasted_iota(jnp.int32, (rows, LANES), 1)


def row_ids():
    return lax.broadcasted_iota(jnp.int32, (8, LANES), 0)


def turned_columns(held, sides, wait):
    group = lane_ids(ROWS) // HALO
    packed = None
    for f in range(4):
        if f in (0, 2):
            wait((f, f + 1))
        for side in sides:
            v = held[3 * f + side, TOP : TOP + ROWS, :]
            shift = (4 * f + 20 * side) % LANES
            v = pltpu.roll(v, shift, 1) if shift else v
            packed = v if packed is None else jnp.where(group == f + 4 * side, v, packed)
    return packed.T


def strips_kernel(water, bed, msg_b, msg_a, own_b, held, sems):
    even = lax.rem(lax.axis_index("gx"), 2) == 0
    copies = []
    for f in range(4):
        for t in range(2):
            cols = pl.ds(t * LANES, LANES)
            src = water.at[f, :, cols] if f < 3 else bed.at[:, cols]
            dst = held.at[3 * f + t, pl.ds(TOP, ROWS), :]
            copies.append(pltpu.make_async_copy(src, dst, sems.at[len(copies)]))
    for copy in copies:
        copy.start()

    def wait(fields):
        for copy in copies[2 * fields[0] : 2 * fields[-1] + 2]:
            copy.wait()

    @pl.when(even)
    def _():
        across = turned_columns(held, (0, 1), wait)
        msg_a[...] = across[16:32, :]
        msg_b[...] = across[0:16, :]
        own_b[...] = across[0:16, :]

    @pl.when(jnp.logical_not(even))
    def _():
        across = turned_columns(held, (1,), wait)
        msg_b[...] = across[16:32, :]
        own_b[...] = across[16:32, :]


def near_kernel(held, msg_in, msg_a):
    @pl.when(lax.rem(lax.axis_index("gx"), 2) == 1)
    def _():
        msg_a[...] = turned_columns(held, (0,), lambda fields: None)[0:16, :]


def ahead_kernel(held, active, rough, factors, known, on_flags, levels, sems):
    gx, nx = lax.axis_index("gx"), lax.axis_size("gx")
    gy, ny = lax.axis_index("gy"), lax.axis_size("gy")
    copies = [
        pltpu.make_async_copy(active, on_flags, sems.at[0]),
        pltpu.make_async_copy(rough, levels, sems.at[1]),
    ]
    for copy in copies:
        copy.start()

    def ahead(c, previous):
        rows = pl.ds(row_of(c), 8)
        load = loader(held, c)
        faces = row_faces(load, range(2))
        over = upper_faces(previous, faces)
        for t in range(2):
            for i in range(3):
                known[2 * i + t, rows, :] = faces[t][i] - over[t][i]
            known[6 + t, rows, :] = drag(*(load(f, t, 0) for f in range(3)))
        return faces

    lax.fori_loop(1, 17, ahead, no_faces(2), unroll=4)
    for copy in copies:
        copy.wait()

    def tile_of(dy, dx):
        row = jnp.clip(gy + dy, 0, ny - 1)
        col = jnp.clip(2 * gx + dx, 0, 2 * nx - 1)
        on = on_flags[0, row, col].astype(jnp.float32)
        level = levels[row, col]
        squares = [DRAG_SCALE * (n * n) for n in MANNING]
        coarse = jnp.where(level == 2, squares[2], squares[3])
        fine = jnp.where(level == 0, squares[0], squares[1])
        return FLUX_SCALE * on, BED_SCALE * on, jnp.where(level < 2, fine, coarse) * on

    def keep(region, values):
        for i, v in enumerate(values):
            factors[3 * region + i] = jnp.broadcast_to(v, (8, LANES))

    rows, low = row_ids(), lane_ids(8) < 64
    for t in range(2):
        own, above, below = tile_of(0, t), tile_of(-1, t), tile_of(1, t)
        keep(OWN[t], own)
        edges = [jnp.where(rows < 4, b, a) for a, b in zip(above, below)]
        outside = jnp.logical_and(rows >= 2, rows < 6)
        keep(EDGES[t], [jnp.where(outside, e, o) for e, o in zip(edges, own)])
    keep(RIM, [jnp.where(low, a, b) for a, b in zip(tile_of(0, 2), tile_of(0, -1))])


def rows_kernel(held, own_b, got_b, got_a, after, msg_b, msg_a, keep_b, upright, stage):
    gx, nx = lax.axis_index("gx"), lax.axis_size("gx")
    even = lax.rem(gx, 2) == 0
    border = jnp.logical_or(gx == 0, gx == nx - 1)
    stage[32:, :] = jnp.zeros((LANES - 32, LANES), jnp.float32)
    for f in range(4):
        a = got_a[4 * f : 4 * f + 4, :]
        b = got_b[4 * f : 4 * f + 4, :]
        sign = -1.0 if f == 1 else 1.0
        mirrored = jnp.concatenate(
            [own_b[4 * f + 3 - k : 4 * f + 4 - k, :] for k in range(4)], axis=0
        )
        b = jnp.where(border, sign * mirrored, b)
        stage[8 * f : 8 * f + 4, :] = jnp.where(even, b, a)
        stage[8 * f + 4 : 8 * f + 8, :] = jnp.where(even, a, b)
    turned = stage[...].T
    upright[...] = turned
    even_y = lax.rem(lax.axis_index("gy"), 2) == 0
    for f in range(4):
        for t in range(3):
            if t == RIM:
                upper = pltpu.roll(turned[0:8, :], 124 - 8 * f, 1)[0:4, :]
                lower = pltpu.roll(turned[120:128, :], 124 - 8 * f, 1)[4:8, :]
            else:
                upper = held[3 * f + t, TOP : TOP + 4, :]
                lower = held[3 * f + t, TOP + 124 : TOP + 128, :]
            at = (pl.ds(4 * f, 4), pl.ds(t * LANES, LANES))
            msg_a[at] = jnp.where(even_y, lower, upper)
            msg_b[at] = jnp.where(even_y, upper, lower)
            keep_b[at] = jnp.where(even_y, upper, lower)


def place_rim(upright, held):
    for f in range(4):
        held[3 * f + RIM, TOP : TOP + ROWS, :] = pltpu.roll(upright[...], 124 - 8 * f, 1)


def side_states(vm, v0, v1, v2):
    d0, d1, d2 = v0 - vm, v1 - v0, v2 - v1
    low, high = jnp.minimum(d1, 0.0), jnp.maximum(d1, 0.0)
    s0 = jnp.minimum(jnp.maximum(d0, low), high)
    s1 = jnp.minimum(jnp.maximum(d2, low), high)
    return v0 + 0.5 * s0, v1 - 0.5 * s1


def side_terms(h, n):
    q = lax.rsqrt(h)
    u = n * (q * q)
    return u, jnp.abs(u) + SQRT_G * (h * q)


def rusanov(left, right):
    (hl, nl, tl), (hr, nr, tr) = left, right
    ul, cl = side_terms(hl, nl)
    ur, cr = side_terms(hr, nr)
    c = jnp.maximum(cl, cr)
    return (
        (nl + nr) - c * (hr - hl),
        (nl * ul + nr * ur) + HALF_G * (hl * hl + hr * hr) - c * (nr - nl),
        (tl * ul + tr * ur) - c * (tr - tl),
    )


def drag(h, p, r):
    square = p * p + r * r
    return square * lax.rsqrt(jnp.maximum(square, SMALLEST)) * jnp.exp(jnp.log(h) * (-7.0 / 3.0))


class Ring:
    def __init__(self):
        lanes = lane_ids(8)
        self.first = lanes == 0
        self.second = lanes < 2
        self.last = lanes == LANES - 1

    def right(self, v, by=1):
        moved = [pltpu.roll(x, by, 1) for x in v]
        edge = self.first if by == 1 else self.second
        return [jnp.where(edge, moved[t - 1], moved[t]) for t in range(3)]

    def left(self, v, count=3):
        moved = [pltpu.roll(x, LANES - 1, 1) for x in v]
        return [jnp.where(self.last, moved[(t + 1) % 3], moved[t]) for t in range(count)]

    def rates(self, h, p, r, count):
        sides = []
        for v in (h, p, r):
            near, far, ahead = self.right(v), self.right(v, 2), self.left(v)
            sides.append([side_states(far[t], near[t], v[t], ahead[t]) for t in range(3)])
        face = [
            rusanov([x[t][0] for x in sides], [x[t][1] for x in sides]) for t in range(3)
        ]
        out = []
        for i in range(3):
            g = [face[t][i] for t in range(3)]
            moved = self.left(g, count)
            out.append([moved[t] - g[t] for t in range(count)])
        return out


def row_faces(load, tiles, shift=0):
    out = []
    for t in tiles:
        sides = [side_states(*(load(f, t, k + shift) for k in (-1, 0, 1, 2))) for f in (0, 2, 1)]
        out.append(rusanov([s[0] for s in sides], [s[1] for s in sides]))
    return out


def no_faces(count):
    return [(jnp.zeros((8, LANES), jnp.float32),) * 3] * count


def upper_faces(previous, faces):
    bottom = row_ids() == 7
    return [
        tuple(pltpu.roll(jnp.where(bottom, a, b), 1, 0) for a, b in zip(p, n))
        for p, n in zip(previous, faces)
    ]


def differences(faces, over):
    return [[n - o for n, o in zip(*pair)] for pair in zip(faces, over)]


def row_of(c):
    return pl.multiple_of(8 * c + TOP - 8, 8)


def loader(ref, c):
    base = row_of(c)
    return lambda f, t, k: ref[3 * f + t, pl.ds(base + k, 8), :]


def pair_of(ref, e, low, high):
    first, then = ref[e, low : low + 8, :], ref[e, high - 4 : high + 4, :]
    return jnp.where(row_ids() < 4, first, then)


def section(ring, load, downs, factors, regions, drags):
    h, p, r, b = ([load(f, t, 0) for t in range(3)] for f in range(4))
    along = ring.rates(h, p, r, 3)
    to_left, to_right = ring.right(b), ring.left(b)
    states, slopes = [], []
    for t in range(3):
        flux, bed, rub = (factors[3 * regions[t] + i] for i in range(3))
        bed_x = bed * (to_right[t] - to_left[t])
        bed_y = bed * (load(3, t, 1) - load(3, t, -1))
        res = rub * (drag(h[t], p[t], r[t]) if drags[t] is None else drags[t])
        down = downs[t]
        states.append(
            (
                h[t] - flux * (along[0][t] + down[0]),
                p[t] - (flux * (along[1][t] + down[2]) + (h[t] * bed_x + res * p[t])),
                r[t] - (flux * (along[2][t] + down[1]) + (h[t] * bed_y + res * r[t])),
            )
        )
        slopes.append((bed_x, bed_y))
    return states, slopes


def result(ring, load, downs, factors, slope_at, start_at):
    h, p, r = ([load(f, t, 0) for t in range(3)] for f in range(3))
    along = ring.rates(h, p, r, 2)
    out = []
    for t in range(2):
        flux, rub = factors[3 * OWN[t]], factors[3 * OWN[t] + 2]
        res = rub * drag(h[t], p[t], r[t])
        down = downs[t]
        change = (
            flux * (along[0][t] + down[0]),
            flux * (along[1][t] + down[2]) + (h[t] * slope_at(t) + res * p[t]),
            flux * (along[2][t] + down[1]) + (h[t] * slope_at(2 + t) + res * r[t]),
        )
        out.append(
            [0.5 * ((start_at(3 * f + t) + v[t]) - change[f]) for f, v in enumerate((h, p, r))]
        )
    return out


def inner_section(held, factors, known, mid, slope):
    ring = Ring()

    def step(c, previous):
        rows = pl.ds(row_of(c), 8)
        load = loader(held, c)
        faces = row_faces(load, [RIM])
        downs = [[known[2 * i + t, rows, :] for i in range(3)] for t in range(2)]
        downs += differences(faces, upper_faces(previous, faces))
        drags = [known[6, rows, :], known[7, rows, :], None]
        states, slopes = section(ring, load, downs, factors, OWN, drags)
        for t in range(3):
            for f in range(3):
                mid[3 * f + t, rows, :] = states[t][f]
            if t != RIM:
                slope[t, rows, :], slope[2 + t, rows, :] = slopes[t]
        return faces

    lax.fori_loop(1, 17, step, no_faces(1), unroll=4)


def inner_result(held, factors, mid, slope, part, first, last):
    ring = Ring()

    def step(c, previous):
        rows = pl.ds(row_of(c), 8)
        load = loader(mid, c)
        faces = row_faces(load, range(2))
        downs = differences(faces, upper_faces(previous, faces))
        values = result(
            ring, load, downs, factors, lambda i: slope[i, rows, :], lambda e: held[e, rows, :]
        )
        place = pl.ds(pl.multiple_of(8 * c - 8, 8), 8)
        for t in range(2):
            for f in range(3):
                part[f, place, pl.ds(t * LANES, LANES)] = values[t][f]
        return faces

    before = no_faces(2) if first == 1 else row_faces(loader(mid, first - 1), range(2))
    lax.fori_loop(first, last + 1, step, before, unroll=4)


def on_parity(parity):
    return pl.when(lax.rem(lax.axis_index("gy"), 2) == parity)


def odd_kernel(held_in, upright, factors, known, msg_in, held, mid, slope, part, msg):
    @on_parity(1)
    def _():
        place_rim(upright, held)
        inner_section(held, factors, known, mid, slope)
        inner_result(held, factors, mid, slope, part, 1, FIRST)


def even_kernel(
    held_in, upright, factors, known, msg_in, mid_in, slope_in, part_in, held, mid, slope, part, msg
):
    @on_parity(0)
    def _():
        place_rim(upright, held)
        inner_section(held, factors, known, mid, slope)
        inner_result(held, factors, mid, slope, part, 1, FIRST)


def rest_kernel(held, factors, mid, slope, part_in, part):
    inner_result(held, factors, mid, slope, part, FIRST + 1, 16)


def outer_kernel(
    held_in, mid_in, slope_in, part, factors, own_b, got_b, got_a, out, held, mid, slope, edge, sems
):
    inner = pl.ds(EDGE, ROWS - 2 * EDGE)
    copies = [pltpu.make_async_copy(part.at[:, inner, :], out.at[:, inner, :], sems.at[0])]
    for i in range(2):
        rows = pl.ds(i * (ROWS - EDGE), EDGE)
        copies.append(pltpu.make_async_copy(edge.at[i], out.at[:, rows, :], sems.at[1 + i]))
    copies[0].start()
    gy, ny = lax.axis_index("gy"), lax.axis_size("gy")
    even_y = lax.rem(gy, 2) == 0
    border = jnp.logical_or(gy == 0, gy == ny - 1)
    for f in range(4):
        for t in range(3):
            cols = slice(t * LANES, (t + 1) * LANES)
            sign = -1.0 if f == 2 else 1.0
            mirrored = jnp.concatenate(
                [own_b[4 * f + 3 - k : 4 * f + 4 - k, cols] for k in range(4)], axis=0
            )
            a = got_a[4 * f : 4 * f + 4, cols]
            b = jnp.where(border, sign * mirrored, got_b[4 * f : 4 * f + 4, cols])
            held[3 * f + t, TOP - 4 : TOP, :] = jnp.where(even_y, b, a)
            held[3 * f + t, TOP + ROWS : TOP + ROWS + 4, :] = jnp.where(even_y, a, b)

    ring = Ring()
    end = TOP + ROWS

    def load(f, t, k):
        return pair_of(held, 3 * f + t, end - 2 + k, TOP - 2 + k)

    downs = differences(row_faces(load, range(3)), row_faces(load, range(3), -1))
    states, slopes = section(ring, load, downs, factors, EDGES, [None] * 3)

    def put(ref, e, v):
        ref[e, end - 2 : end + 2, :] = v[0:4, :]
        ref[e, TOP - 2 : TOP + 2, :] = v[4:8, :]

    for t in range(3):
        for f in range(3):
            put(mid, 3 * f + t, states[t][f])
        if t != RIM:
            put(slope, t, slopes[t][0])
            put(slope, 2 + t, slopes[t][1])

    def load_mid(f, t, k):
        return pair_of(mid, 3 * f + t, end - 4 + k, TOP + k)

    downs = differences(row_faces(load_mid, range(2)), row_faces(load_mid, range(2), -1))
    values = result(
        ring,
        load_mid,
        downs,
        factors,
        lambda i: pair_of(slope, i, end - 4, TOP),
        lambda e: pair_of(held, e, end - 4, TOP),
    )
    upper = row_ids() < 4
    for t in range(2):
        cols = pl.ds(t * LANES, LANES)
        for f in range(3):
            v = pltpu.roll(values[t][f], 4, 0)
            edge[0, f, :, cols] = jnp.where(upper, v, part[f, 0:EDGE, cols])
            edge[1, f, :, cols] = jnp.where(upper, part[f, ROWS - EDGE : ROWS, cols], v)
    for copy in copies[1:]:
        copy.start()
    for copy in copies:
        copy.wait()


def call(kernel, outs, specs, scratch=(), aliases=None, room=4, cost=0, out_specs=None):
    shapes = [jax.ShapeDtypeStruct(s, jnp.float32) for s in outs]
    return pl.pallas_call(
        kernel,
        out_shape=shapes,
        in_specs=specs,
        out_specs=out_specs or [VMEM] * len(shapes),
        scratch_shapes=scratch,
        input_output_aliases=aliases or {},
        compiler_params=pltpu.CompilerParams(vmem_limit_bytes=room << 20),
        cost_estimate=pl.CostEstimate(flops=cost, bytes_accessed=cost, transcendentals=0),
    )


def body(water, bed, active, rough):
    col_b, col_a, own_col, held = call(
        strips_kernel,
        [STRIP, STRIP, STRIP, HELD],
        [HBM] * 2,
        [pltpu.SemaphoreType.DMA((8,))],
    )(*(pltpu.with_memory_space_constraint(x, pltpu.HBM) for x in (water, bed)))
    got_b = swap(col_b, "gx", 1)
    col_a = call(near_kernel, [STRIP], [VMEM] * 2, aliases={1: 0}, cost=1_000_000)(held, col_a)[0]
    got_a = swap(col_a, "gx", 0)
    factors, known = call(
        ahead_kernel,
        [FACTORS, KNOWN],
        [VMEM, HBM, HBM],
        [
            pltpu.SMEM((1, 16, 64), jnp.int32),
            pltpu.SMEM((16, 64), jnp.int32),
            pltpu.SemaphoreType.DMA((2,)),
        ],
        cost=4_000_000,
    )(held, *(pltpu.with_memory_space_constraint(x, pltpu.HBM) for x in (active, rough)))
    row_b, row_a, own_row, upright = call(
        rows_kernel,
        [BAND, BAND, BAND, (ROWS, LANES)],
        [VMEM] * 5,
        [pltpu.VMEM((LANES, LANES), jnp.float32)],
    )(held, own_col, got_b, got_a, factors)
    held, mid, slope, part, row_b = call(
        odd_kernel,
        [HELD, MID, SLOPE, BLOCK, BAND],
        [VMEM] * 5,
        aliases={0: 0, 4: 4},
        room=8,
        cost=10_000_000,
    )(held, upright, factors, known, row_b)
    down_b = swap(row_b, "gy", 1)
    held, mid, slope, part, row_a = call(
        even_kernel,
        [HELD, MID, SLOPE, BLOCK, BAND],
        [VMEM] * 8,
        aliases={0: 0, 5: 1, 6: 2, 7: 3, 4: 4},
        room=8,
        cost=10_000_000,
    )(held, upright, factors, known, row_a, mid, slope, part)
    down_a = swap(row_a, "gy", 0)
    part = call(rest_kernel, [BLOCK], [VMEM] * 5, aliases={4: 0}, room=8, cost=10_000_000)(
        held, factors, mid, slope, part
    )[0]
    return call(
        outer_kernel,
        [BLOCK, HELD, MID, SLOPE],
        [VMEM] * 8,
        [pltpu.VMEM((2, 3, EDGE, 2 * LANES), jnp.float32), pltpu.SemaphoreType.DMA((3,))],
        aliases={0: 1, 1: 2, 2: 3},
        room=8,
        out_specs=[HBM] + [VMEM] * 3,
    )(held, mid, slope, part, factors, own_row, down_b, down_a)[0]


def solution(mesh):
    return jax.shard_map(
        body,
        mesh=mesh,
        in_specs=(P(None, "gy", "gx"), P("gy", "gx"), P(), P()),
        out_specs=P(None, "gy", "gx"),
        check_vma=False,
    )
```

```python
import jax
import jax.numpy as jnp
from jax import lax
from jax.experimental import pallas as pl
from jax.experimental.pallas import tpu as pltpu
from jax.sharding import PartitionSpec as P


GRAVITY = 9.81
SPACING = 2.0
TIME_STEP = 0.1
MANNING = (0.03, 0.06, 0.1, 0.15)

LANES = 128
ROWS = 128
HALO = 4
TOP = 16
STAGED = ROWS + 2 * TOP
RIM = 2
SQRT_G = GRAVITY**0.5
HALF_G = 0.5 * GRAVITY
FLUX_SCALE = 0.5 * TIME_STEP / SPACING
BED_SCALE = TIME_STEP * GRAVITY / (2.0 * SPACING)
DRAG_SCALE = TIME_STEP * GRAVITY
SMALLEST = 1.1754944e-38

OWN, EDGES = (0, 1, 2), (3, 4, 2)
REGIONS = 5

VMEM = pl.BlockSpec(memory_space=pltpu.VMEM)
HBM = pl.BlockSpec(memory_space=pltpu.HBM)

HELD = (12, STAGED, LANES)
MID = (9, STAGED, LANES)
SLOPE = (4, STAGED, LANES)
KNOWN = (8, STAGED, LANES)
FACTORS = (3 * REGIONS, 8, LANES)
STRIP = (16, LANES)
BAND = (16, 3 * LANES)
BLOCK = (3, ROWS, 2 * LANES)
EDGE = 8
FIRST = 5


def swap(x, axis, odd):
    n = lax.axis_size(axis)
    pairs = []
    for i in range(odd, n - 1, 2):
        pairs += [(i, i + 1), (i + 1, i)]
    return lax.ppermute(x, axis, pairs)


def lane_ids(rows):
    return lax.broadcasted_iota(jnp.int32, (rows, LANES), 1)


def row_ids():
    return lax.broadcasted_iota(jnp.int32, (8, LANES), 0)


def strips_kernel(water, bed, msg_b, msg_a, own_b, held, sems):
    even = lax.rem(lax.axis_index("gx"), 2) == 0
    copies = []
    for f in range(4):
        for t in range(2):
            cols = pl.ds(t * LANES, LANES)
            src = water.at[f, :, cols] if f < 3 else bed.at[:, cols]
            dst = held.at[3 * f + t, pl.ds(TOP, ROWS), :]
            copies.append(pltpu.make_async_copy(src, dst, sems.at[len(copies)]))
    for copy in copies:
        copy.start()
    group = lane_ids(ROWS) // HALO
    packed = None
    for f in range(4):
        if f in (0, 2):
            for copy in copies[2 * f : 2 * f + 4]:
                copy.wait()
        for side in range(2):
            v = held[3 * f + side, TOP : TOP + ROWS, :]
            shift = (4 * f + 20 * side) % LANES
            v = pltpu.roll(v, shift, 1) if shift else v
            packed = v if packed is None else jnp.where(group == f + 4 * side, v, packed)
    across = packed.T
    left, right = across[0:16, :], across[16:32, :]
    msg_a[...] = jnp.where(even, right, left)
    msg_b[...] = jnp.where(even, left, right)
    own_b[...] = jnp.where(even, left, right)


def ahead_kernel(held, active, rough, factors, known, on_flags, levels, sems):
    gx, nx = lax.axis_index("gx"), lax.axis_size("gx")
    gy, ny = lax.axis_index("gy"), lax.axis_size("gy")
    copies = [
        pltpu.make_async_copy(active, on_flags, sems.at[0]),
        pltpu.make_async_copy(rough, levels, sems.at[1]),
    ]
    for copy in copies:
        copy.start()

    def ahead(c, previous):
        rows = pl.ds(row_of(c), 8)
        load = loader(held, c)
        faces = row_faces(load, range(2))
        over = upper_faces(previous, faces)
        for t in range(2):
            for i in range(3):
                known[2 * i + t, rows, :] = faces[t][i] - over[t][i]
            known[6 + t, rows, :] = drag(*(load(f, t, 0) for f in range(3)))
        return faces

    lax.fori_loop(1, 17, ahead, no_faces(2), unroll=4)
    for copy in copies:
        copy.wait()

    def tile_of(dy, dx):
        row = jnp.clip(gy + dy, 0, ny - 1)
        col = jnp.clip(2 * gx + dx, 0, 2 * nx - 1)
        on = on_flags[0, row, col].astype(jnp.float32)
        level = levels[row, col]
        squares = [DRAG_SCALE * (n * n) for n in MANNING]
        coarse = jnp.where(level == 2, squares[2], squares[3])
        fine = jnp.where(level == 0, squares[0], squares[1])
        return FLUX_SCALE * on, BED_SCALE * on, jnp.where(level < 2, fine, coarse) * on

    def keep(region, values):
        for i, v in enumerate(values):
            factors[3 * region + i] = jnp.broadcast_to(v, (8, LANES))

    rows, low = row_ids(), lane_ids(8) < 64
    for t in range(2):
        own, above, below = tile_of(0, t), tile_of(-1, t), tile_of(1, t)
        keep(OWN[t], own)
        edges = [jnp.where(rows < 4, b, a) for a, b in zip(above, below)]
        outside = jnp.logical_and(rows >= 2, rows < 6)
        keep(EDGES[t], [jnp.where(outside, e, o) for e, o in zip(edges, own)])
    keep(RIM, [jnp.where(low, a, b) for a, b in zip(tile_of(0, 2), tile_of(0, -1))])


def rows_kernel(held, own_b, got_b, got_a, after, msg_b, msg_a, keep_b, upright, stage):
    gx, nx = lax.axis_index("gx"), lax.axis_size("gx")
    even = lax.rem(gx, 2) == 0
    border = jnp.logical_or(gx == 0, gx == nx - 1)
    stage[32:, :] = jnp.zeros((LANES - 32, LANES), jnp.float32)
    for f in range(4):
        a = got_a[4 * f : 4 * f + 4, :]
        b = got_b[4 * f : 4 * f + 4, :]
        sign = -1.0 if f == 1 else 1.0
        mirrored = jnp.concatenate(
            [own_b[4 * f + 3 - k : 4 * f + 4 - k, :] for k in range(4)], axis=0
        )
        b = jnp.where(border, sign * mirrored, b)
        stage[8 * f : 8 * f + 4, :] = jnp.where(even, b, a)
        stage[8 * f + 4 : 8 * f + 8, :] = jnp.where(even, a, b)
    turned = stage[...].T
    upright[...] = turned
    even_y = lax.rem(lax.axis_index("gy"), 2) == 0
    for f in range(4):
        for t in range(3):
            if t == RIM:
                upper = pltpu.roll(turned[0:8, :], 124 - 8 * f, 1)[0:4, :]
                lower = pltpu.roll(turned[120:128, :], 124 - 8 * f, 1)[4:8, :]
            else:
                upper = held[3 * f + t, TOP : TOP + 4, :]
                lower = held[3 * f + t, TOP + 124 : TOP + 128, :]
            at = (pl.ds(4 * f, 4), pl.ds(t * LANES, LANES))
            msg_a[at] = jnp.where(even_y, lower, upper)
            msg_b[at] = jnp.where(even_y, upper, lower)
            keep_b[at] = jnp.where(even_y, upper, lower)


def place_rim(upright, held):
    for f in range(4):
        held[3 * f + RIM, TOP : TOP + ROWS, :] = pltpu.roll(upright[...], 124 - 8 * f, 1)


def side_states(vm, v0, v1, v2):
    d0, d1, d2 = v0 - vm, v1 - v0, v2 - v1
    low, high = jnp.minimum(d1, 0.0), jnp.maximum(d1, 0.0)
    s0 = jnp.minimum(jnp.maximum(d0, low), high)
    s1 = jnp.minimum(jnp.maximum(d2, low), high)
    return v0 + 0.5 * s0, v1 - 0.5 * s1


def side_terms(h, n):
    q = lax.rsqrt(h)
    u = n * (q * q)
    return u, jnp.abs(u) + SQRT_G * (h * q)


def rusanov(left, right):
    (hl, nl, tl), (hr, nr, tr) = left, right
    ul, cl = side_terms(hl, nl)
    ur, cr = side_terms(hr, nr)
    c = jnp.maximum(cl, cr)
    return (
        (nl + nr) - c * (hr - hl),
        (nl * ul + nr * ur) + HALF_G * (hl * hl + hr * hr) - c * (nr - nl),
        (tl * ul + tr * ur) - c * (tr - tl),
    )


def drag(h, p, r):
    square = p * p + r * r
    return square * lax.rsqrt(jnp.maximum(square, SMALLEST)) * jnp.exp(jnp.log(h) * (-7.0 / 3.0))


class Ring:
    def __init__(self):
        lanes = lane_ids(8)
        self.first = lanes == 0
        self.second = lanes < 2
        self.last = lanes == LANES - 1

    def right(self, v, by=1):
        moved = [pltpu.roll(x, by, 1) for x in v]
        edge = self.first if by == 1 else self.second
        return [jnp.where(edge, moved[t - 1], moved[t]) for t in range(3)]

    def left(self, v, count=3):
        moved = [pltpu.roll(x, LANES - 1, 1) for x in v]
        return [jnp.where(self.last, moved[(t + 1) % 3], moved[t]) for t in range(count)]

    def rates(self, h, p, r, count):
        sides = []
        for v in (h, p, r):
            near, far, ahead = self.right(v), self.right(v, 2), self.left(v)
            sides.append([side_states(far[t], near[t], v[t], ahead[t]) for t in range(3)])
        face = [
            rusanov([x[t][0] for x in sides], [x[t][1] for x in sides]) for t in range(3)
        ]
        out = []
        for i in range(3):
            g = [face[t][i] for t in range(3)]
            moved = self.left(g, count)
            out.append([moved[t] - g[t] for t in range(count)])
        return out


def row_faces(load, tiles, shift=0):
    out = []
    for t in tiles:
        sides = [side_states(*(load(f, t, k + shift) for k in (-1, 0, 1, 2))) for f in (0, 2, 1)]
        out.append(rusanov([s[0] for s in sides], [s[1] for s in sides]))
    return out


def no_faces(count):
    return [(jnp.zeros((8, LANES), jnp.float32),) * 3] * count


def upper_faces(previous, faces):
    bottom = row_ids() == 7
    return [
        tuple(pltpu.roll(jnp.where(bottom, a, b), 1, 0) for a, b in zip(p, n))
        for p, n in zip(previous, faces)
    ]


def differences(faces, over):
    return [[n - o for n, o in zip(*pair)] for pair in zip(faces, over)]


def row_of(c):
    return pl.multiple_of(8 * c + TOP - 8, 8)


def loader(ref, c):
    base = row_of(c)
    return lambda f, t, k: ref[3 * f + t, pl.ds(base + k, 8), :]


def pair_of(ref, e, low, high):
    first, then = ref[e, low : low + 8, :], ref[e, high - 4 : high + 4, :]
    return jnp.where(row_ids() < 4, first, then)


def section(ring, load, downs, factors, regions, drags):
    h, p, r, b = ([load(f, t, 0) for t in range(3)] for f in range(4))
    along = ring.rates(h, p, r, 3)
    to_left, to_right = ring.right(b), ring.left(b)
    states, slopes = [], []
    for t in range(3):
        flux, bed, rub = (factors[3 * regions[t] + i] for i in range(3))
        bed_x = bed * (to_right[t] - to_left[t])
        bed_y = bed * (load(3, t, 1) - load(3, t, -1))
        res = rub * (drag(h[t], p[t], r[t]) if drags[t] is None else drags[t])
        down = downs[t]
        states.append(
            (
                h[t] - flux * (along[0][t] + down[0]),
                p[t] - (flux * (along[1][t] + down[2]) + (h[t] * bed_x + res * p[t])),
                r[t] - (flux * (along[2][t] + down[1]) + (h[t] * bed_y + res * r[t])),
            )
        )
        slopes.append((bed_x, bed_y))
    return states, slopes


def result(ring, load, downs, factors, slope_at, start_at):
    h, p, r = ([load(f, t, 0) for t in range(3)] for f in range(3))
    along = ring.rates(h, p, r, 2)
    out = []
    for t in range(2):
        flux, rub = factors[3 * OWN[t]], factors[3 * OWN[t] + 2]
        res = rub * drag(h[t], p[t], r[t])
        down = downs[t]
        change = (
            flux * (along[0][t] + down[0]),
            flux * (along[1][t] + down[2]) + (h[t] * slope_at(t) + res * p[t]),
            flux * (along[2][t] + down[1]) + (h[t] * slope_at(2 + t) + res * r[t]),
        )
        out.append(
            [0.5 * ((start_at(3 * f + t) + v[t]) - change[f]) for f, v in enumerate((h, p, r))]
        )
    return out


def inner_section(held, factors, known, mid, slope):
    ring = Ring()

    def step(c, previous):
        rows = pl.ds(row_of(c), 8)
        load = loader(held, c)
        faces = row_faces(load, [RIM])
        downs = [[known[2 * i + t, rows, :] for i in range(3)] for t in range(2)]
        downs += differences(faces, upper_faces(previous, faces))
        drags = [known[6, rows, :], known[7, rows, :], None]
        states, slopes = section(ring, load, downs, factors, OWN, drags)
        for t in range(3):
            for f in range(3):
                mid[3 * f + t, rows, :] = states[t][f]
            if t != RIM:
                slope[t, rows, :], slope[2 + t, rows, :] = slopes[t]
        return faces

    lax.fori_loop(1, 17, step, no_faces(1), unroll=4)


def inner_result(held, factors, mid, slope, part, first, last):
    ring = Ring()

    def step(c, previous):
        rows = pl.ds(row_of(c), 8)
        load = loader(mid, c)
        faces = row_faces(load, range(2))
        downs = differences(faces, upper_faces(previous, faces))
        values = result(
            ring, load, downs, factors, lambda i: slope[i, rows, :], lambda e: held[e, rows, :]
        )
        place = pl.ds(pl.multiple_of(8 * c - 8, 8), 8)
        for t in range(2):
            for f in range(3):
                part[f, place, pl.ds(t * LANES, LANES)] = values[t][f]
        return faces

    before = no_faces(2) if first == 1 else row_faces(loader(mid, first - 1), range(2))
    lax.fori_loop(first, last + 1, step, before, unroll=4)


def on_parity(parity):
    return pl.when(lax.rem(lax.axis_index("gy"), 2) == parity)


def odd_kernel(held_in, upright, factors, known, msg_in, held, mid, slope, part, msg):
    @on_parity(1)
    def _():
        place_rim(upright, held)
        inner_section(held, factors, known, mid, slope)
        inner_result(held, factors, mid, slope, part, 1, FIRST)


def even_kernel(
    held_in, upright, factors, known, msg_in, mid_in, slope_in, part_in, held, mid, slope, part, msg
):
    @on_parity(0)
    def _():
        place_rim(upright, held)
        inner_section(held, factors, known, mid, slope)
        inner_result(held, factors, mid, slope, part, 1, FIRST)


def rest_kernel(held, factors, mid, slope, part_in, part):
    inner_result(held, factors, mid, slope, part, FIRST + 1, 16)


def outer_kernel(
    held_in, mid_in, slope_in, part, factors, own_b, got_b, got_a, out, held, mid, slope, edge, sems
):
    inner = pl.ds(EDGE, ROWS - 2 * EDGE)
    copies = [pltpu.make_async_copy(part.at[:, inner, :], out.at[:, inner, :], sems.at[0])]
    for i in range(2):
        rows = pl.ds(i * (ROWS - EDGE), EDGE)
        copies.append(pltpu.make_async_copy(edge.at[i], out.at[:, rows, :], sems.at[1 + i]))
    copies[0].start()
    gy, ny = lax.axis_index("gy"), lax.axis_size("gy")
    even_y = lax.rem(gy, 2) == 0
    border = jnp.logical_or(gy == 0, gy == ny - 1)
    for f in range(4):
        for t in range(3):
            cols = slice(t * LANES, (t + 1) * LANES)
            sign = -1.0 if f == 2 else 1.0
            mirrored = jnp.concatenate(
                [own_b[4 * f + 3 - k : 4 * f + 4 - k, cols] for k in range(4)], axis=0
            )
            a = got_a[4 * f : 4 * f + 4, cols]
            b = jnp.where(border, sign * mirrored, got_b[4 * f : 4 * f + 4, cols])
            held[3 * f + t, TOP - 4 : TOP, :] = jnp.where(even_y, b, a)
            held[3 * f + t, TOP + ROWS : TOP + ROWS + 4, :] = jnp.where(even_y, a, b)

    ring = Ring()
    end = TOP + ROWS

    def load(f, t, k):
        return pair_of(held, 3 * f + t, end - 2 + k, TOP - 2 + k)

    downs = differences(row_faces(load, range(3)), row_faces(load, range(3), -1))
    states, slopes = section(ring, load, downs, factors, EDGES, [None] * 3)

    def put(ref, e, v):
        ref[e, end - 2 : end + 2, :] = v[0:4, :]
        ref[e, TOP - 2 : TOP + 2, :] = v[4:8, :]

    for t in range(3):
        for f in range(3):
            put(mid, 3 * f + t, states[t][f])
        if t != RIM:
            put(slope, t, slopes[t][0])
            put(slope, 2 + t, slopes[t][1])

    def load_mid(f, t, k):
        return pair_of(mid, 3 * f + t, end - 4 + k, TOP + k)

    downs = differences(row_faces(load_mid, range(2)), row_faces(load_mid, range(2), -1))
    values = result(
        ring,
        load_mid,
        downs,
        factors,
        lambda i: pair_of(slope, i, end - 4, TOP),
        lambda e: pair_of(held, e, end - 4, TOP),
    )
    upper = row_ids() < 4
    for t in range(2):
        cols = pl.ds(t * LANES, LANES)
        for f in range(3):
            v = pltpu.roll(values[t][f], 4, 0)
            edge[0, f, :, cols] = jnp.where(upper, v, part[f, 0:EDGE, cols])
            edge[1, f, :, cols] = jnp.where(upper, part[f, ROWS - EDGE : ROWS, cols], v)
    for copy in copies[1:]:
        copy.start()
    for copy in copies:
        copy.wait()


def call(kernel, outs, specs, scratch=(), aliases=None, room=4, cost=0, out_specs=None):
    shapes = [jax.ShapeDtypeStruct(s, jnp.float32) for s in outs]
    return pl.pallas_call(
        kernel,
        out_shape=shapes,
        in_specs=specs,
        out_specs=out_specs or [VMEM] * len(shapes),
        scratch_shapes=scratch,
        input_output_aliases=aliases or {},
        compiler_params=pltpu.CompilerParams(vmem_limit_bytes=room << 20),
        cost_estimate=pl.CostEstimate(flops=cost, bytes_accessed=cost, transcendentals=0),
    )


def body(water, bed, active, rough):
    col_b, col_a, own_col, held = call(
        strips_kernel,
        [STRIP, STRIP, STRIP, HELD],
        [HBM] * 2,
        [pltpu.SemaphoreType.DMA((8,))],
    )(*(pltpu.with_memory_space_constraint(x, pltpu.HBM) for x in (water, bed)))
    got_b = swap(col_b, "gx", 1)
    got_a = swap(col_a, "gx", 0)
    factors, known = call(
        ahead_kernel,
        [FACTORS, KNOWN],
        [VMEM, HBM, HBM],
        [
            pltpu.SMEM((1, 16, 64), jnp.int32),
            pltpu.SMEM((16, 64), jnp.int32),
            pltpu.SemaphoreType.DMA((2,)),
        ],
        cost=4_000_000,
    )(held, *(pltpu.with_memory_space_constraint(x, pltpu.HBM) for x in (active, rough)))
    row_b, row_a, own_row, upright = call(
        rows_kernel,
        [BAND, BAND, BAND, (ROWS, LANES)],
        [VMEM] * 5,
        [pltpu.VMEM((LANES, LANES), jnp.float32)],
    )(held, own_col, got_b, got_a, factors)
    held, mid, slope, part, row_b = call(
        odd_kernel,
        [HELD, MID, SLOPE, BLOCK, BAND],
        [VMEM] * 5,
        aliases={0: 0, 4: 4},
        room=8,
        cost=10_000_000,
    )(held, upright, factors, known, row_b)
    down_b = swap(row_b, "gy", 1)
    held, mid, slope, part, row_a = call(
        even_kernel,
        [HELD, MID, SLOPE, BLOCK, BAND],
        [VMEM] * 8,
        aliases={0: 0, 5: 1, 6: 2, 7: 3, 4: 4},
        room=8,
        cost=10_000_000,
    )(held, upright, factors, known, row_a, mid, slope, part)
    down_a = swap(row_a, "gy", 0)
    part = call(rest_kernel, [BLOCK], [VMEM] * 5, aliases={4: 0}, room=8, cost=10_000_000)(
        held, factors, mid, slope, part
    )[0]
    return call(
        outer_kernel,
        [BLOCK, HELD, MID, SLOPE],
        [VMEM] * 8,
        [pltpu.VMEM((2, 3, EDGE, 2 * LANES), jnp.float32), pltpu.SemaphoreType.DMA((3,))],
        aliases={0: 1, 1: 2, 2: 3},
        room=8,
        out_specs=[HBM] + [VMEM] * 3,
    )(held, mid, slope, part, factors, own_row, down_b, down_a)[0]


def solution(mesh):
    return jax.shard_map(
        body,
        mesh=mesh,
        in_specs=(P(None, "gy", "gx"), P("gy", "gx"), P(), P()),
        out_specs=P(None, "gy", "gx"),
        check_vma=False,
    )
```
